768 devices in a mesh: dp: 24 (over z, core), fsdp: 32 (over x, y).
Axes of the slice: x: 4, y: 8, z: 12, core: 2. Of those that a mesh axis runs over, the one named last changes fastest.
Arguments:
- inputs: bfloat16 [12288, 8192], P('dp', 'fsdp'), may hold values from -6 to 6
- cotangent: bfloat16 [2, 12288, 1024], P(None, 'dp', 'fsdp'), may hold values from -0.29882812 to 0.29882812
- feedback: float32 [2, 24, 8192, 1024], P(None, 'dp', 'fsdp'), may hold values from -6 to 6
- q_init: float32 [2, 1024, 128], replicated, may hold values from -0.1875 to 0.1875
- factor_ranks: int32 [2], replicated, may hold values from 8 to 128, as said below
Outputs:
- factor_p: float32 [2, 8192, 128], P(None, 'fsdp')
- factor_q: float32 [2, 1024, 128], replicated
- new_error: float32 [2, 24, 8192, 1024], P(None, 'dp', 'fsdp')
The draws below stay inside these ranges and needn't reach their ends.
Inputs may be any that keep to these rules, and one draw needn't show every extreme that they name: `factor_ranks`: some projection has rank 128.
All inputs are finite; a program needn't handle non-finite values.
Results may differ from the reference program's by a relative error of at most 0.0003.
Values may be sent and summed in bfloat16 or wider, within the bound.
A program may use at most 32 MiB of HBM per device.

```python
import jax
import jax.numpy as jnp
from jax import lax

D = 8192
KV = 1024
RMAX = 128
TOK_DEV = 512
REPLICAS = 24
TOKENS = 12288
N_DP = 24


def draw_factor_ranks(key, part):
    subkeys = jax.random.split(jax.random.fold_in(key, 11), 2)
    other_ranks = jax.random.randint(subkeys[0], (2,), 8, RMAX + 1)
    chosen = jax.random.randint(subkeys[1], (), 0, 2)
    return jnp.where(jnp.arange(2) == chosen, RMAX, other_ranks).astype(jnp.int32)


def level_of(own_key, shape, pieces, least, top_value):
    level = 1.0
    for position, shards_of in pieces:
        heights = jax.random.uniform(jax.random.fold_in(jax.random.fold_in(own_key, 6), position), (shards_of,), jnp.float32, least / len(pieces), top_value / len(pieces))
        level = level * jnp.repeat(jnp.exp(heights), shape[position] // shards_of).reshape((-1,) + (1,) * (len(shape) - 1 - position))
    return level


def noise(key, shape, scale, reach, cuts=(), held_as=jnp.bfloat16):
    factor_of = level_of(key, shape, cuts, -0.22, 0.18) if cuts else 1.0
    drawn = jax.random.normal(key, shape, jnp.float32) * scale * factor_of
    return jnp.minimum(jnp.maximum(drawn, -reach), reach).astype(held_as)


def setup_inputs(seed: int = 0) -> dict:
    splits = jax.random.split(jax.random.key(seed), 6)
    return {
        "inputs": noise(splits[0], (TOKENS, D), 1.0, 6.0, ((0, 24), (1, 32))),
        "cotangent": noise(splits[1], (2, TOKENS, KV), 0.05, 0.29882812, ((1, 24), (2, 32))),
        "feedback": noise(splits[2], (2, REPLICAS, D, KV), 1.0, 6.0, ((1, 24), (2, 32)), jnp.float32),
        "q_init": noise(splits[3], (2, KV, RMAX), KV ** -0.5, 0.1875, (), jnp.float32),
        "factor_ranks": draw_factor_ranks(jax.random.fold_in(splits[5], 71), 0),
    }


PRECISE = lax.Precision.HIGHEST

def triangle_solve(lower_factor, right_side):
    return jax.scipy.linalg.solve_triangular(lower_factor, right_side, lower=True)

def reference(inputs, cotangent, feedback, q_init, factor_ranks):
    input_split = inputs.astype(jnp.float32).reshape(N_DP, TOK_DEV, D)
    cotan_split = cotangent.astype(jnp.float32).reshape(2, N_DP, TOK_DEV, KV)
    rank_mask = (jnp.arange(RMAX)[None, :] < factor_ranks[:, None]).astype(jnp.float32)
    masked_q = q_init * rank_mask[:, None, :]

    def full_of(replica):
        input_rows = lax.dynamic_index_in_dim(input_split, replica, 0, keepdims=False)
        cotan_rows = lax.dynamic_index_in_dim(cotan_split, replica, 1, keepdims=False)
        feedback_rows = lax.dynamic_index_in_dim(feedback, replica, 1, keepdims=False)
        return feedback_rows + jnp.einsum('td,mtk->mdk', input_rows, cotan_rows, precision=PRECISE)

    def add_left(running, replica):
        return (running + jnp.einsum('mdk,mkr->mdr', full_of(replica), masked_q, precision=PRECISE), None)
    left_sum, _ = lax.scan(add_left, jnp.zeros((2, D, RMAX), jnp.float32), jnp.arange(N_DP))
    gram_matrix = jnp.einsum('mdr,mds->mrs', left_sum, left_sum, precision=PRECISE)
    gram_matrix = gram_matrix + jax.vmap(jnp.diag)(1.0 - rank_mask)
    chol_lower = jnp.linalg.cholesky(gram_matrix)
    solved = jax.vmap(triangle_solve)(chol_lower, jnp.swapaxes(left_sum, 1, 2))
    factor_p = jnp.swapaxes(solved, 1, 2)

    def add_right(running, replica):
        return (running + jnp.einsum('mdk,mdr->mkr', full_of(replica), factor_p, precision=PRECISE), None)
    factor_q, _ = lax.scan(add_right, jnp.zeros((2, KV, RMAX), jnp.float32), jnp.arange(N_DP))
    low_rank = jnp.einsum('mdr,mkr->mdk', factor_p, factor_q, precision=PRECISE)
    per_replica = lax.map(lambda replica: full_of(replica) - low_rank, jnp.arange(N_DP))
    new_error = jnp.swapaxes(per_replica, 0, 1)
    return (factor_p, factor_q, new_error)
```

```python
import functools

import jax
import jax.numpy as jnp
from jax import lax
from jax.experimental import pallas as pl
from jax.experimental.pallas import tpu as pltpu
from jax.sharding import Mesh
from jax.sharding import PartitionSpec as P

MESH = pl.DeviceIdType.MESH
HI = lax.Precision.HIGHEST
NZ, NX, NY = 12, 4, 8
NF = NX * NY
PIECE = 24
DP = ("z", "c")
FS = ("x", "y")

OFFS = sorted(
    [(dx, dy) for dx in range(NX) for dy in range(NY) if dx or dy],
    key=lambda o: -(min(o[0], NX - o[0]) + min(o[1], NY - o[1])),
)
ZOFFS = sorted(range(1, NZ), key=lambda d: -min(d, NZ - d))


def nt(a, b, precision=HI):
    return lax.dot_general(
        a, b, (((1,), (1,)), ((), ())), precision=precision, preferred_element_type=jnp.float32
    )


def nn(a, b, precision=HI):
    return lax.dot_general(
        a, b, (((1,), (0,)), ((), ())), precision=precision, preferred_element_type=jnp.float32
    )


def comm_kernel(
    ranks, x_hbm, cot_hbm, fb_hbm, q_hbm,
    g_out, s_out, pf_out, li_out,
    xb, cv, cs, ct, fb, qv, gx, cf_t, pp, rs, pf3, s_src, s_rs, s_z, gl, g_rs, gg, mat,
    l_sem, pr_send, pr_recv, a_send, a_recv, b_send, b_recv, z_send, z_recv, f_send, f_recv,
):
    z, c, x, y = (lax.axis_index(n) for n in ("z", "c", "x", "y"))
    oc = 1 - c
    f = x * NY + y
    pending = []

    def at(dz=0, dx=0, dy=0):
        return (lax.rem(z + dz, NZ), c, lax.rem(x + dx, NX), lax.rem(y + dy, NY))

    partner = (z, oc, x, y)

    def send(src, dst, ssem, rsem, dev):
        cp = pltpu.make_async_remote_copy(
            src_ref=src, dst_ref=dst, send_sem=ssem, recv_sem=rsem, device_id=dev, device_id_type=MESH
        )
        cp.start()
        pending.append(cp)

    def arrive(dst, ssem, rsem, dev):
        pltpu.make_async_remote_copy(
            src_ref=dst, dst_ref=dst, send_sem=ssem, recv_sem=rsem, device_id=dev, device_id_type=MESH
        ).wait_recv()

    barrier = pltpu.get_barrier_semaphore()
    peers = [partner] + [at(dx=dx, dy=dy) for dx, dy in OFFS] + [at(dz=d) for d in ZOFFS]
    for peer in peers:
        pl.semaphore_signal(barrier, inc=1, device_id=peer, device_id_type=MESH)

    load_c = pltpu.make_async_copy(cot_hbm, cv, l_sem.at[0])
    load_x = pltpu.make_async_copy(x_hbm, xb.at[c], l_sem.at[1])
    load_f = pltpu.make_async_copy(fb_hbm.at[c, 0], fb.at[c], l_sem.at[2])
    load_q = pltpu.make_async_copy(q_hbm.at[c], qv, l_sem.at[3])
    load_c.start()
    load_x.start()
    load_f.start()
    load_q.start()

    load_c.wait()
    ct[c, x, y] = cv[c].astype(jnp.float32).T.astype(jnp.bfloat16)
    cs[...] = cv[oc].astype(jnp.float32).T.astype(jnp.bfloat16)

    pl.semaphore_wait(barrier, len(peers))

    send(cs, ct.at[c, x, y], pr_send.at[0], pr_recv.at[0], partner)

    def chunk(r, dx, dy):
        return ct.at[r, lax.rem(x + dx + NX, NX), lax.rem(y + dy + NY, NY)]

    def a_y(dirn, s):
        k = chunk(c, 0, -dirn * (s - 1))
        i = (s - 1) if dirn > 0 else 3 + s
        send(k, k, a_send.at[i], a_recv.at[i], at(dy=dirn % NY))

    def a_y_wait(dirn, s):
        i = (s - 1) if dirn > 0 else 3 + s
        arrive(chunk(c, 0, -dirn * s), a_send.at[i], a_recv.at[i], at(dy=-dirn % NY))

    def a_x(j, dirn):
        k = chunk(c, 0, -j)
        i = 8 + j * 3 + (0 if dirn > 0 else 1)
        send(k, k, a_send.at[i], a_recv.at[i], at(dx=dirn % NX))

    def a_x_wait(j, dirn):
        i = 8 + j * 3 + (0 if dirn > 0 else 1)
        arrive(chunk(c, -dirn, -j), a_send.at[i], a_recv.at[i], at(dx=-dirn % NX))

    def far_dir(j):
        return 1 if j % 2 == 0 else -1

    def a_x_far(j):
        d = far_dir(j)
        k = chunk(c, -d, -j)
        i = 8 + j * 3 + 2
        send(k, k, a_send.at[i], a_recv.at[i], at(dx=d % NX))

    def a_x_far_wait(j):
        d = far_dir(j)
        i = 8 + j * 3 + 2
        arrive(chunk(c, -2 * d, -j), a_send.at[i], a_recv.at[i], at(dx=-d % NX))

    def b_x(dx):
        k = chunk(oc, 0, 0)
        send(k, k, b_send.at[dx - 1], b_recv.at[dx - 1], at(dx=dx))

    def b_x_wait(dx):
        arrive(chunk(oc, -dx, 0), b_send.at[dx - 1], b_recv.at[dx - 1], at(dx=NX - dx))

    def b_reach(dx, dirn):
        return (4 if dirn > 0 else 3) if dx % 2 == 0 else (3 if dirn > 0 else 4)

    def b_idx(dx, dirn, s):
        return 3 + dx * 8 + (s - 1 if dirn > 0 else 3 + s)

    def b_y(dx, dirn, s):
        k = chunk(oc, -dx, -dirn * (s - 1))
        i = b_idx(dx, dirn, s)
        send(k, k, b_send.at[i], b_recv.at[i], at(dy=dirn % NY))

    def b_y_wait(dx, dirn, s):
        i = b_idx(dx, dirn, s)
        arrive(chunk(oc, -dx, -dirn * s), b_send.at[i], b_recv.at[i], at(dy=-dirn % NY))

    a_y(1, 1)
    a_y(-1, 1)
    a_x(0, 1)
    a_x(0, -1)

    arrive(ct.at[oc, x, y], pr_send.at[0], pr_recv.at[0], partner)
    for dx in (1, 3, 2):
        b_x(dx)
    b_y(0, 1, 1)
    b_y(0, -1, 1)
    load_x.wait()
    send(xb.at[c], xb.at[c], pr_send.at[1], pr_recv.at[1], partner)
    send(fb_hbm.at[oc, 0], fb.at[c], pr_send.at[2], pr_recv.at[2], partner)

    def y_of(j):
        return j

    a_x_done = []
    for s in range(1, 5):
        a_y_wait(1, s)
        if s < 4:
            a_y(1, s + 1)
        a_x(s, 1)
        a_x(s, -1)
        if s < 4:
            a_y_wait(-1, s)
            if s < 3:
                a_y(-1, s + 1)
            a_x(NY - s, 1)
            a_x(NY - s, -1)
        if s == 1:
            for dx in (1, 3, 2):
                b_x_wait(dx)
                b_y(dx, 1, 1)
                b_y(dx, -1, 1)
        for dx in (0, 1, 3, 2):
            for dirn in (1, -1):
                if s <= b_reach(dx, dirn):
                    b_y_wait(dx, dirn, s)
                    if s < b_reach(dx, dirn):
                        b_y(dx, dirn, s + 1)
        ready = {1: (0,), 2: (1, 7), 3: (2, 6), 4: (3, 5)}[s]
        for j in ready:
            d = far_dir(j)
            a_x_wait(j, d)
            a_x_far(j)
            a_x_wait(j, -d)
            a_x_done.append(j)
    d = far_dir(4)
    a_x_wait(4, d)
    a_x_far(4)
    a_x_wait(4, -d)
    for j in (0, 1, 7, 2, 6, 3, 5, 4):
        a_x_far_wait(j)

    load_f.wait()
    arrive(xb.at[oc], pr_send.at[1], pr_recv.at[1], partner)
    arrive(fb.at[oc], pr_send.at[2], pr_recv.at[2], partner)
    x_own = xb[c].astype(jnp.float32).T.astype(jnp.bfloat16)
    x_oth = xb[oc].astype(jnp.float32).T.astype(jnp.bfloat16)
    load_q.wait()
    width = lax.broadcasted_iota(jnp.int32, (1, 128), 1)
    rank = ranks[c]
    live = width < rank
    total = jnp.zeros((256, 128), jnp.float32)
    for b in range(NX):
        cols = pl.ds(b * 256, 256)
        own = fb[c, :, cols] + nt(x_own, ct[c, b].reshape(256, 512), None)
        oth = fb[oc, :, cols] + nt(x_oth, ct[oc, b].reshape(256, 512), None)
        g_out[c, :, cols] = own
        gx[:, cols] = oth
        both = own + oth
        total = total + nn(both, jnp.where(live, qv[cols, :], 0.0))
        cf_t[cols, :] = both.T
    for i in range(NZ):
        lo, hi = i * PIECE, min((i + 1) * PIECE, 256)
        if hi - lo == PIECE:
            pp[i] = total[lo:hi]
        elif hi > lo:
            pp[i, : hi - lo] = total[lo:hi]
            pp[i, hi - lo :] = jnp.zeros((PIECE - (hi - lo), 128), jnp.float32)
        else:
            pp[i] = jnp.zeros((PIECE, 128), jnp.float32)

    for d in ZOFFS:
        send(pp.at[lax.rem(z + d, NZ)], rs.at[d], z_send.at[d], z_recv.at[d], at(dz=d))
    send(gx, g_out.at[c], pr_send.at[3], pr_recv.at[3], partner)
    acc = pp[z]
    for d in reversed(ZOFFS):
        arrive(rs.at[d], z_send.at[d], z_recv.at[d], at(dz=NZ - d))
        acc = acc + rs[d]
    pf3[z] = acc
    for d in ZOFFS:
        send(pf3.at[z], pf3.at[z], z_send.at[12 + d], z_recv.at[12 + d], at(dz=d))
    for d in reversed(ZOFFS):
        zs = lax.rem(z + NZ - d, NZ)
        arrive(pf3.at[zs], z_send.at[12 + d], z_recv.at[12 + d], at(dz=NZ - d))
    left = pf3[...].reshape(NZ * PIECE, 128)[:256]
    pf_out[c] = left
    send(pf_out.at[c], pf_out.at[c], pr_send.at[4], pr_recv.at[4], partner)

    gram = nn(left.T, left)
    for i in range(NF):
        gl[i] = gram[4 * i : 4 * i + 4]
    for n, (dx, dy) in enumerate(OFFS):
        to = lax.rem(x + dx, NX) * NY + lax.rem(y + dy, NY)
        send(gl.at[to], g_rs.at[n], f_send.at[n], f_recv.at[n], at(dx=dx, dy=dy))
    for b in range(NX):
        rows = pl.ds(b * 256, 256)
        s_src[pl.ds(b * NY, NY)] = nn(cf_t[rows, :], left).reshape(NY, 32, 128)
    for n, (dx, dy) in enumerate(OFFS):
        to = lax.rem(x + dx, NX) * NY + lax.rem(y + dy, NY)
        send(s_src.at[to], s_rs.at[n], f_send.at[32 + n], f_recv.at[32 + n], at(dx=dx, dy=dy))

    def src(dx, dy):
        return at(dx=(NX - dx) % NX, dy=(NY - dy) % NY)

    acc = gl[f]
    for n, (dx, dy) in reversed(list(enumerate(OFFS))):
        arrive(g_rs.at[n], f_send.at[n], f_recv.at[n], src(dx, dy))
        acc = acc + g_rs[n]
    gg[f] = acc
    for n, (dx, dy) in enumerate(OFFS):
        send(gg.at[f], gg.at[f], f_send.at[64 + n], f_recv.at[64 + n], at(dx=dx, dy=dy))

    acc = s_src[f]
    for n, (dx, dy) in reversed(list(enumerate(OFFS))):
        arrive(s_rs.at[n], f_send.at[32 + n], f_recv.at[32 + n], src(dx, dy))
        acc = acc + s_rs[n]
    s_z[z] = acc
    for d in ZOFFS:
        send(s_z.at[z], s_z.at[z], z_send.at[24 + d], z_recv.at[24 + d], at(dz=d))

    for n, (dx, dy) in reversed(list(enumerate(OFFS))):
        sx, sy = lax.rem(x + NX - dx, NX), lax.rem(y + NY - dy, NY)
        arrive(gg.at[sx * NY + sy], f_send.at[64 + n], f_recv.at[64 + n], src(dx, dy))
    for i in range(NF):
        mat[4 * i : 4 * i + 4, :] = gg[i]
    row_id = lax.broadcasted_iota(jnp.int32, (128, 128), 0)
    col_id = lax.broadcasted_iota(jnp.int32, (128, 128), 1)
    mat[...] = mat[...] + jnp.where((row_id == col_id) & (col_id >= rank), 1.0, 0.0)

    def eliminate(j, carry):
        m = mat[...]
        row = mat[pl.ds(j, 1), :]
        hit = col_id == j
        hit1 = width == j
        pivot = jnp.sum(jnp.where(hit1, row, 0.0), axis=1, keepdims=True)
        col = jnp.sum(jnp.where(hit, m, 0.0), axis=1, keepdims=True)
        factor = jnp.where(row_id > j, col / pivot, 0.0)
        mat[...] = jnp.where(hit & (row_id > j), 0.0, m) - factor * jnp.where(hit1, 1.0, row)
        return carry

    lax.fori_loop(0, 64, eliminate, 0)

    for d in reversed(ZOFFS):
        zs = lax.rem(z + NZ - d, NZ)
        arrive(s_z.at[zs], z_send.at[24 + d], z_recv.at[24 + d], at(dz=NZ - d))
    acc = s_z[0]
    for i in range(1, NZ):
        acc = acc + s_z[i]
    s_out[c, f] = acc
    for n, (dx, dy) in enumerate(OFFS):
        send(s_out.at[c, f], s_out.at[c, f], f_send.at[96 + n], f_recv.at[96 + n], at(dx=dx, dy=dy))

    lax.fori_loop(64, 128, eliminate, 0)
    m = mat[...]
    diag = jnp.sum(jnp.where(row_id == col_id, m, 0.0), axis=1, keepdims=True)
    unit = jnp.where(row_id == col_id, 1.0, jnp.where(row_id > col_id, m, 0.0))
    li_out[c] = unit * (1.0 / jnp.sqrt(diag))
    send(li_out.at[c], li_out.at[c], pr_send.at[5], pr_recv.at[5], partner)

    for n, (dx, dy) in reversed(list(enumerate(OFFS))):
        sx, sy = lax.rem(x + NX - dx, NX), lax.rem(y + NY - dy, NY)
        arrive(s_out.at[c, sx * NY + sy], f_send.at[96 + n], f_recv.at[96 + n], src(dx, dy))
    send(s_out.at[c], s_out.at[c], pr_send.at[6], pr_recv.at[6], partner)
    arrive(g_out.at[oc], pr_send.at[3], pr_recv.at[3], partner)
    arrive(pf_out.at[oc], pr_send.at[4], pr_recv.at[4], partner)
    arrive(li_out.at[oc], pr_send.at[5], pr_recv.at[5], partner)
    arrive(s_out.at[oc], pr_send.at[6], pr_recv.at[6], partner)
    for cp in pending:
        cp.wait_send()


def final_kernel(g, s, pf, li, p_out, q_out, e_out):
    inv = li[0]
    left = nt(pf[0], inv)
    p_out[0] = left
    for b in range(4):
        rows = pl.ds(b * 256, 256)
        right = nt(s[0, rows, :], inv)
        q_out[0, rows, :] = right
        e_out[0, 0, :, rows] = g[0, :, rows] - nt(left, right)


def local(inputs, cotangent, feedback, q_init, factor_ranks):
    f32, b16 = jnp.float32, jnp.bfloat16
    vm = pl.BlockSpec(memory_space=pltpu.VMEM)
    anyspace = pl.BlockSpec(memory_space=pl.ANY)
    dma = pltpu.SemaphoreType.DMA
    g, s, pf, li = pl.pallas_call(
        comm_kernel,
        out_shape=(
            jax.ShapeDtypeStruct((2, 256, 1024), f32),
            jax.ShapeDtypeStruct((2, NF, 32, 128), f32),
            jax.ShapeDtypeStruct((2, 256, 128), f32),
            jax.ShapeDtypeStruct((2, 128, 128), f32),
        ),
        in_specs=[pl.BlockSpec(memory_space=pltpu.SMEM)] + [anyspace] * 4,
        out_specs=(vm,) * 4,
        scratch_shapes=[
            pltpu.VMEM((2, 512, 256), b16),
            pltpu.VMEM((2, 512, 32), b16),
            pltpu.VMEM((32, 512), b16),
            pltpu.VMEM((2, NX, NY, 32, 512), b16),
            pltpu.VMEM((2, 256, 1024), f32),
            pltpu.VMEM((1024, 128), f32),
            pltpu.VMEM((256, 1024), f32),
            pltpu.VMEM((1024, 256), f32),
            pltpu.VMEM((NZ, PIECE, 128), f32),
            pltpu.VMEM((NZ, PIECE, 128), f32),
            pltpu.VMEM((NZ, PIECE, 128), f32),
            pltpu.VMEM((NF, 32, 128), f32),
            pltpu.VMEM((NF, 32, 128), f32),
            pltpu.VMEM((NZ, 32, 128), f32),
            pltpu.VMEM((NF, 4, 128), f32),
            pltpu.VMEM((NF, 4, 128), f32),
            pltpu.VMEM((NF, 4, 128), f32),
            pltpu.VMEM((128, 128), f32),
            dma((4,)),
            dma((7,)), dma((7,)),
            dma((32,)), dma((32,)),
            dma((35,)), dma((35,)),
            dma((36,)), dma((36,)),
            dma((128,)), dma((128,)),
        ],
        compiler_params=pltpu.CompilerParams(
            collective_id=0, has_side_effects=True, vmem_limit_bytes=56 << 20
        ),
        name="exchange",
    )(factor_ranks, inputs, cotangent, feedback, q_init)
    s = s.reshape(2, 1024, 128)

    def whole(*shape):
        return pl.BlockSpec((1, *shape), lambda m: (m,) + (0,) * len(shape))

    return pl.pallas_call(
        final_kernel,
        grid=(2,),
        out_shape=(
            jax.ShapeDtypeStruct((2, 256, 128), f32),
            jax.ShapeDtypeStruct((2, 1024, 128), f32),
            jax.ShapeDtypeStruct((2, 1, 256, 1024), f32),
        ),
        in_specs=[whole(256, 1024), whole(1024, 128), whole(256, 128), whole(128, 128)],
        out_specs=(whole(256, 128), whole(1024, 128), whole(1, 256, 1024)),
        compiler_params=pltpu.CompilerParams(dimension_semantics=("arbitrary",)),
        name="finish",
    )(g, s, pf, li)


def solution(mesh):
    torus = Mesh(mesh.devices.reshape(NZ, 2, NX, NY), ("z", "c", "x", "y"))
    placed = (P(DP, FS), P(None, DP, FS), P(None, DP, FS, None), P(), P())
    return jax.shard_map(
        local,
        mesh=torus,
        in_specs=placed,
        out_specs=(P(None, FS, None), P(), P(None, DP, FS, None)),
        check_vma=False,
    )
```

```python
import functools

import jax
import jax.numpy as jnp
from jax import lax
from jax.experimental import pallas as pl
from jax.experimental.pallas import tpu as pltpu
from jax.sharding import Mesh
from jax.sharding import PartitionSpec as P

MESH = pl.DeviceIdType.MESH
HI = lax.Precision.HIGHEST
NZ, NX, NY = 12, 4, 8
NF = NX * NY
PIECE = 24
DP = ("z", "c")
FS = ("x", "y")

OFFS = sorted(
    [(dx, dy) for dx in range(NX) for dy in range(NY) if dx or dy],
    key=lambda o: -(min(o[0], NX - o[0]) + min(o[1], NY - o[1])),
)
ZOFFS = sorted(range(1, NZ), key=lambda d: -min(d, NZ - d))


def nt(a, b, precision=HI):
    return lax.dot_general(
        a, b, (((1,), (1,)), ((), ())), precision=precision, preferred_element_type=jnp.float32
    )


def nn(a, b, precision=HI):
    return lax.dot_general(
        a, b, (((1,), (0,)), ((), ())), precision=precision, preferred_element_type=jnp.float32
    )


def split(a):
    high = a.astype(jnp.bfloat16)
    return high, (a - high.astype(jnp.float32)).astype(jnp.bfloat16)


def three(dot, a, b):
    (ah, al), (bh, bl) = a, b
    return dot(ah, bh, None) + (dot(ah, bl, None) + dot(al, bh, None))


def comm_kernel(
    ranks, x_hbm, cot_hbm, fb_hbm, q_hbm,
    g_out, s_out, pf_out, li_out,
    xb, ct, fb, qv, gw, gx, cf_h, cf_l, pp, rs, pf3, s_src, s_rs, s_z, gl, g_rs, gg, mat,
    l_sem, pr_send, pr_recv, a_send, a_recv, b_send, b_recv, z_send, z_recv, f_send, f_recv, near,
):
    z, c, x, y = (lax.axis_index(n) for n in ("z", "c", "x", "y"))
    oc = 1 - c
    f = x * NY + y
    pending = []

    def at(dz=0, dx=0, dy=0):
        return (lax.rem(z + dz, NZ), c, lax.rem(x + dx, NX), lax.rem(y + dy, NY))

    partner = (z, oc, x, y)

    def send(src, dst, ssem, rsem, dev):
        cp = pltpu.make_async_remote_copy(
            src_ref=src, dst_ref=dst, send_sem=ssem, recv_sem=rsem, device_id=dev, device_id_type=MESH
        )
        cp.start()
        pending.append(cp)

    def arrive(dst, ssem, rsem, dev):
        pltpu.make_async_remote_copy(
            src_ref=dst, dst_ref=dst, send_sem=ssem, recv_sem=rsem, device_id=dev, device_id_type=MESH
        ).wait_recv()

    barrier = pltpu.get_barrier_semaphore()
    peers = [partner] + [(z, oc, lax.rem(x + dx, NX), y) for dx in (1, 2, 3)]
    peers += [at(dx=1), at(dx=NX - 1), at(dy=1), at(dy=NY - 1), at(dz=1), at(dz=NZ - 1)]
    for peer in peers:
        pl.semaphore_signal(barrier, inc=1, device_id=peer, device_id_type=MESH)

    load_c = pltpu.make_async_copy(cot_hbm.at[c], ct.at[c, x, y], l_sem.at[0])
    load_x = pltpu.make_async_copy(x_hbm, xb.at[c], l_sem.at[1])
    load_f = pltpu.make_async_copy(fb_hbm.at[c, 0], fb.at[c], l_sem.at[2])
    load_q = pltpu.make_async_copy(q_hbm.at[c], qv, l_sem.at[3])
    load_c.start()
    load_x.start()
    load_f.start()
    load_q.start()
    load_c.wait()
    load_x.wait()

    pl.semaphore_wait(barrier, len(peers))

    def tell(r):
        for n, dz in enumerate((1, NZ - 1)):
            pl.semaphore_signal(near.at[r - 1, n], inc=1, device_id=at(dz=dz), device_id_type=MESH)

    def told(r):
        for n in range(2):
            pl.semaphore_wait(near.at[r - 1, n], 1)

    def chunk(r, dx, dy):
        return ct.at[r, lax.rem(x + dx + NX, NX), lax.rem(y + dy + NY, NY)]

    def a_y(dirn, s):
        k = chunk(c, 0, -dirn * (s - 1))
        i = (s - 1) if dirn > 0 else 3 + s
        send(k, k, a_send.at[i], a_recv.at[i], at(dy=dirn % NY))

    def a_y_wait(dirn, s):
        i = (s - 1) if dirn > 0 else 3 + s
        arrive(chunk(c, 0, -dirn * s), a_send.at[i], a_recv.at[i], at(dy=-dirn % NY))

    def a_x(j, dirn):
        k = chunk(c, 0, -j)
        i = 8 + j * 3 + (0 if dirn > 0 else 1)
        send(k, k, a_send.at[i], a_recv.at[i], at(dx=dirn % NX))

    def a_x_wait(j, dirn):
        i = 8 + j * 3 + (0 if dirn > 0 else 1)
        arrive(chunk(c, -dirn, -j), a_send.at[i], a_recv.at[i], at(dx=-dirn % NX))

    def far_dir(j):
        return 1 if j % 2 == 0 else -1

    def a_x_far(j):
        d = far_dir(j)
        k = chunk(c, -d, -j)
        i = 8 + j * 3 + 2
        send(k, k, a_send.at[i], a_recv.at[i], at(dx=d % NX))

    def a_x_far_wait(j):
        d = far_dir(j)
        i = 8 + j * 3 + 2
        arrive(chunk(c, -2 * d, -j), a_send.at[i], a_recv.at[i], at(dx=-d % NX))

    def b_x(dx):
        send(cot_hbm.at[oc], ct.at[c, x, y], b_send.at[dx], b_recv.at[dx], (z, oc, lax.rem(x + dx, NX), y))

    def b_x_wait(dx):
        arrive(chunk(oc, -dx, 0), b_send.at[dx], b_recv.at[dx], partner)

    def b_reach(dx, dirn):
        return (4 if dirn > 0 else 3) if dx % 2 == 0 else (3 if dirn > 0 else 4)

    def b_idx(dx, dirn, s):
        return 4 + dx * 8 + (s - 1 if dirn > 0 else 3 + s)

    def b_y(dx, dirn, s):
        k = chunk(oc, -dx, -dirn * (s - 1))
        i = b_idx(dx, dirn, s)
        send(k, k, b_send.at[i], b_recv.at[i], at(dy=dirn % NY))

    def b_y_wait(dx, dirn, s):
        i = b_idx(dx, dirn, s)
        arrive(chunk(oc, -dx, -dirn * s), b_send.at[i], b_recv.at[i], at(dy=-dirn % NY))

    a_y(1, 1)
    a_y(-1, 1)
    a_x(0, 1)
    a_x(0, -1)

    for dx in (0, 1, 3, 2):
        b_x(dx)
    tell(1)
    b_x_wait(0)
    b_y(0, 1, 1)
    b_y(0, -1, 1)
    send(xb.at[c], xb.at[c], pr_send.at[1], pr_recv.at[1], partner)
    send(fb_hbm.at[oc, 0], fb.at[c], pr_send.at[2], pr_recv.at[2], partner)

    for s in range(1, 5):
        a_y_wait(1, s)
        if s < 4:
            a_y(1, s + 1)
        a_x(s, 1)
        a_x(s, -1)
        if s < 4:
            a_y_wait(-1, s)
            if s < 3:
                a_y(-1, s + 1)
            a_x(NY - s, 1)
            a_x(NY - s, -1)
        if s == 1:
            for dx in (1, 3, 2):
                b_x_wait(dx)
                b_y(dx, 1, 1)
                b_y(dx, -1, 1)
        for dx in (0, 1, 3, 2):
            for dirn in (1, -1):
                if s <= b_reach(dx, dirn):
                    b_y_wait(dx, dirn, s)
                    if s < b_reach(dx, dirn):
                        b_y(dx, dirn, s + 1)
        told(s)
        tell(s + 1)
        ready = {1: (0,), 2: (1, 7), 3: (2, 6), 4: (3, 5)}[s]
        for j in ready:
            d = far_dir(j)
            a_x_wait(j, d)
            a_x_far(j)
            a_x_wait(j, -d)
    d = far_dir(4)
    a_x_wait(4, d)
    a_x_far(4)
    a_x_wait(4, -d)
    told(5)
    arrive(xb.at[oc], pr_send.at[1], pr_recv.at[1], partner)
    arrive(fb.at[oc], pr_send.at[2], pr_recv.at[2], partner)
    load_f.wait()
    load_q.wait()
    x_own = xb[c].astype(jnp.float32).T.astype(jnp.bfloat16)
    x_oth = xb[oc].astype(jnp.float32).T.astype(jnp.bfloat16)
    for j in (0, 1, 7, 2, 6, 3, 5, 4):
        a_x_far_wait(j)

    width = lax.broadcasted_iota(jnp.int32, (1, 128), 1)
    rank = ranks[c]
    live = width < rank
    total = jnp.zeros((256, 128), jnp.float32)
    for b in range(NX):
        cols = pl.ds(b * 256, 256)
        own = fb[c, :, cols] + nt(x_own, ct[c, b].reshape(256, 512), None)
        oth = fb[oc, :, cols] + nt(x_oth, ct[oc, b].reshape(256, 512), None)
        gw[:, cols] = own
        gx[:, cols] = oth
        both = own + oth
        total = total + three(nn, split(both), split(jnp.where(live, qv[cols, :], 0.0)))
    for i in range(NZ):
        lo, hi = i * PIECE, min((i + 1) * PIECE, 256)
        if hi - lo == PIECE:
            pp[i] = total[lo:hi]
        elif hi > lo:
            pp[i, : hi - lo] = total[lo:hi]
            pp[i, hi - lo :] = jnp.zeros((PIECE - (hi - lo), 128), jnp.float32)
        else:
            pp[i] = jnp.zeros((PIECE, 128), jnp.float32)

    for d in ZOFFS:
        send(pp.at[lax.rem(z + d, NZ)], rs.at[d], z_send.at[d], z_recv.at[d], at(dz=d))
    send(gx, g_out.at[c], pr_send.at[3], pr_recv.at[3], partner)
    keep_g = pltpu.make_async_copy(gw, g_out.at[c], l_sem.at[4])
    keep_g.start()
    for b in range(NX):
        cols = pl.ds(b * 256, 256)
        cf_h[cols, :], cf_l[cols, :] = split((gw[:, cols] + gx[:, cols]).T)
    acc = pp[z]
    for d in reversed(ZOFFS):
        arrive(rs.at[d], z_send.at[d], z_recv.at[d], at(dz=NZ - d))
        acc = acc + rs[d]
    pf3[z] = acc
    for d in ZOFFS:
        send(pf3.at[z], pf3.at[z], z_send.at[12 + d], z_recv.at[12 + d], at(dz=d))
    for d in reversed(ZOFFS):
        zs = lax.rem(z + NZ - d, NZ)
        arrive(pf3.at[zs], z_send.at[12 + d], z_recv.at[12 + d], at(dz=NZ - d))
    left = pf3[...].reshape(NZ * PIECE, 128)[:256]
    pf_out[c] = left
    send(pf_out.at[c], pf_out.at[c], pr_send.at[4], pr_recv.at[4], partner)

    gram = nn(left.T, left)
    for i in range(NF):
        gl[i] = gram[4 * i : 4 * i + 4]
    for n, (dx, dy) in enumerate(OFFS):
        to = lax.rem(x + dx, NX) * NY + lax.rem(y + dy, NY)
        send(gl.at[to], g_rs.at[n], f_send.at[n], f_recv.at[n], at(dx=dx, dy=dy))
    left_parts = split(left)
    for b in range(NX):
        rows = pl.ds(b * 256, 256)
        s_src[pl.ds(b * NY, NY)] = three(nn, (cf_h[rows, :], cf_l[rows, :]), left_parts).reshape(NY, 32, 128)
    for n, (dx, dy) in enumerate(OFFS):
        to = lax.rem(x + dx, NX) * NY + lax.rem(y + dy, NY)
        send(s_src.at[to], s_rs.at[n], f_send.at[32 + n], f_recv.at[32 + n], at(dx=dx, dy=dy))

    def src(dx, dy):
        return at(dx=(NX - dx) % NX, dy=(NY - dy) % NY)

    acc = gl[f]
    for n, (dx, dy) in reversed(list(enumerate(OFFS))):
        arrive(g_rs.at[n], f_send.at[n], f_recv.at[n], src(dx, dy))
        acc = acc + g_rs[n]
    gg[f] = acc
    for n, (dx, dy) in enumerate(OFFS):
        send(gg.at[f], gg.at[f], f_send.at[64 + n], f_recv.at[64 + n], at(dx=dx, dy=dy))

    acc = s_src[f]
    for n, (dx, dy) in reversed(list(enumerate(OFFS))):
        arrive(s_rs.at[n], f_send.at[32 + n], f_recv.at[32 + n], src(dx, dy))
        acc = acc + s_rs[n]
    s_z[z] = acc
    for d in ZOFFS:
        send(s_z.at[z], s_z.at[z], z_send.at[24 + d], z_recv.at[24 + d], at(dz=d))

    for n, (dx, dy) in reversed(list(enumerate(OFFS))):
        sx, sy = lax.rem(x + NX - dx, NX), lax.rem(y + NY - dy, NY)
        arrive(gg.at[sx * NY + sy], f_send.at[64 + n], f_recv.at[64 + n], src(dx, dy))
    for i in range(NF):
        mat[4 * i : 4 * i + 4, :] = gg[i]
    row_id = lax.broadcasted_iota(jnp.int32, (128, 128), 0)
    col_id = lax.broadcasted_iota(jnp.int32, (128, 128), 1)
    mat[...] = mat[...] + jnp.where((row_id == col_id) & (col_id >= rank), 1.0, 0.0)

    def eliminate(j, carry):
        m = mat[...]
        row = mat[pl.ds(j, 1), :]
        hit = col_id == j
        hit1 = width == j
        pivot = jnp.sum(jnp.where(hit1, row, 0.0), axis=1, keepdims=True)
        col = jnp.sum(jnp.where(hit, m, 0.0), axis=1, keepdims=True)
        factor = jnp.where(row_id > j, col / pivot, 0.0)
        mat[...] = jnp.where(hit & (row_id > j), 0.0, m) - factor * jnp.where(hit1, 1.0, row)
        return carry

    lax.fori_loop(0, 64, eliminate, 0)

    for d in reversed(ZOFFS):
        zs = lax.rem(z + NZ - d, NZ)
        arrive(s_z.at[zs], z_send.at[24 + d], z_recv.at[24 + d], at(dz=NZ - d))
    acc = s_z[0]
    for i in range(1, NZ):
        acc = acc + s_z[i]
    s_out[c, f] = acc

    def forward(k, i):
        send(s_out.at[c, k], s_out.at[c, k], f_send.at[128 + i], f_recv.at[128 + i], partner)

    for n, (dx, dy) in enumerate(OFFS):
        send(s_out.at[c, f], s_out.at[c, f], f_send.at[96 + n], f_recv.at[96 + n], at(dx=dx, dy=dy))

    lax.fori_loop(64, 128, eliminate, 0)
    m = mat[...]
    diag = jnp.sum(jnp.where(row_id == col_id, m, 0.0), axis=1, keepdims=True)
    unit = jnp.where(row_id == col_id, 1.0, jnp.where(row_id > col_id, m, 0.0))
    li_out[c] = unit * (1.0 / jnp.sqrt(diag))
    send(li_out.at[c], li_out.at[c], pr_send.at[5], pr_recv.at[5], partner)

    forward(f, NF - 1)
    for n, (dx, dy) in reversed(list(enumerate(OFFS))):
        k = lax.rem(x + NX - dx, NX) * NY + lax.rem(y + NY - dy, NY)
        arrive(s_out.at[c, k], f_send.at[96 + n], f_recv.at[96 + n], src(dx, dy))
        forward(k, n)
    keep_g.wait()
    arrive(g_out.at[oc], pr_send.at[3], pr_recv.at[3], partner)
    arrive(pf_out.at[oc], pr_send.at[4], pr_recv.at[4], partner)
    arrive(li_out.at[oc], pr_send.at[5], pr_recv.at[5], partner)
    arrive(s_out.at[oc, f], f_send.at[128 + NF - 1], f_recv.at[128 + NF - 1], partner)
    for n, (dx, dy) in reversed(list(enumerate(OFFS))):
        k = lax.rem(x + NX - dx, NX) * NY + lax.rem(y + NY - dy, NY)
        arrive(s_out.at[oc, k], f_send.at[128 + n], f_recv.at[128 + n], partner)
    for cp in pending:
        cp.wait_send()


def final_kernel(g, s, pf, li, p_out, q_out, e_out, left_h, left_l):
    inv = split(li[0])

    @pl.when(pl.program_id(1) == 0)
    def _():
        left = three(nt, split(pf[0]), inv)
        p_out[0] = left
        left_h[...], left_l[...] = split(left)

    right = three(nt, split(s[0]), inv)
    q_out[0] = right
    e_out[0, 0] = g[0] - three(nt, (left_h[...], left_l[...]), split(right))


def local(inputs, cotangent, feedback, q_init, factor_ranks):
    f32, b16 = jnp.float32, jnp.bfloat16
    vm = pl.BlockSpec(memory_space=pltpu.VMEM)
    anyspace = pl.BlockSpec(memory_space=pl.ANY)
    dma = pltpu.SemaphoreType.DMA
    g, s, pf, li = pl.pallas_call(
        comm_kernel,
        out_shape=(
            jax.ShapeDtypeStruct((2, 256, 1024), f32),
            jax.ShapeDtypeStruct((2, NF, 32, 128), f32),
            jax.ShapeDtypeStruct((2, 256, 128), f32),
            jax.ShapeDtypeStruct((2, 128, 128), f32),
        ),
        in_specs=[pl.BlockSpec(memory_space=pltpu.SMEM)] + [anyspace] * 4,
        out_specs=(anyspace, vm, vm, vm),
        scratch_shapes=[
            pltpu.VMEM((2, 512, 256), b16),
            pltpu.VMEM((2, NX, NY, 32, 512), b16),
            pltpu.VMEM((2, 256, 1024), f32),
            pltpu.VMEM((1024, 128), f32),
            pltpu.VMEM((256, 1024), f32),
            pltpu.VMEM((256, 1024), f32),
            pltpu.VMEM((1024, 256), b16),
            pltpu.VMEM((1024, 256), b16),
            pltpu.VMEM((NZ, PIECE, 128), f32),
            pltpu.VMEM((NZ, PIECE, 128), f32),
            pltpu.VMEM((NZ, PIECE, 128), f32),
            pltpu.VMEM((NF, 32, 128), f32),
            pltpu.VMEM((NF, 32, 128), f32),
            pltpu.VMEM((NZ, 32, 128), f32),
            pltpu.VMEM((NF, 4, 128), f32),
            pltpu.VMEM((NF, 4, 128), f32),
            pltpu.VMEM((NF, 4, 128), f32),
            pltpu.VMEM((128, 128), f32),
            dma((5,)),
            dma((7,)), dma((7,)),
            dma((32,)), dma((32,)),
            dma((36,)), dma((36,)),
            dma((36,)), dma((36,)),
            dma((160,)), dma((160,)),
            pltpu.SemaphoreType.REGULAR((5, 2)),
        ],
        compiler_params=pltpu.CompilerParams(
            collective_id=0, has_side_effects=True, vmem_limit_bytes=56 << 20
        ),
        name="exchange",
    )(factor_ranks, inputs, jnp.swapaxes(cotangent, 1, 2), feedback, q_init)
    s = s.reshape(2, 1024, 128)

    def whole(*shape):
        return pl.BlockSpec((1, *shape), lambda m, b: (m,) + (0,) * len(shape))

    blocks = 4
    width = 1024 // blocks
    rows = pl.BlockSpec((1, width, 128), lambda m, b: (m, b, 0))
    return pl.pallas_call(
        final_kernel,
        grid=(2, blocks),
        out_shape=(
            jax.ShapeDtypeStruct((2, 256, 128), f32),
            jax.ShapeDtypeStruct((2, 1024, 128), f32),
            jax.ShapeDtypeStruct((2, 1, 256, 1024), f32),
        ),
        in_specs=[
            pl.BlockSpec((1, 256, width), lambda m, b: (m, 0, b)), rows, whole(256, 128), whole(128, 128),
        ],
        out_specs=(whole(256, 128), rows, pl.BlockSpec((1, 1, 256, width), lambda m, b: (m, 0, 0, b))),
        scratch_shapes=[pltpu.VMEM((256, 128), b16)] * 2,
        compiler_params=pltpu.CompilerParams(dimension_semantics=("arbitrary", "arbitrary")),
        name="finish",
    )(g, s, pf, li)


def solution(mesh):
    torus = Mesh(mesh.devices.reshape(NZ, 2, NX, NY), ("z", "c", "x", "y"))
    placed = (P(DP, FS), P(None, DP, FS), P(None, DP, FS, None), P(), P())
    return jax.shard_map(
        local,
        mesh=torus,
        in_specs=placed,
        out_specs=(P(None, FS, None), P(), P(None, DP, FS, None)),
        check_vma=False,
    )
```

```python
import functools

import jax
import jax.numpy as jnp
from jax import lax
from jax.experimental import pallas as pl
from jax.experimental.pallas import tpu as pltpu
from jax.sharding import Mesh
from jax.sharding import PartitionSpec as P

MESH = pl.DeviceIdType.MESH
HI = lax.Precision.HIGHEST
NZ, NX, NY = 12, 4, 8
NF = NX * NY
STEPS = (48, 80)
PIECE = 24
DP = ("z", "c")
FS = ("x", "y")

OFFS = sorted(
    [(dx, dy) for dx in range(NX) for dy in range(NY) if dx or dy],
    key=lambda o: -(min(o[0], NX - o[0]) + min(o[1], NY - o[1])),
)
YOFFS = (4, 3, 5, 2, 6, 1, 7)
ZOFFS = sorted(range(1, NZ), key=lambda d: -min(d, NZ - d))


def nt(a, b, precision=HI):
    return lax.dot_general(
        a, b, (((1,), (1,)), ((), ())), precision=precision, preferred_element_type=jnp.float32
    )


def nn(a, b, precision=HI):
    return lax.dot_general(
        a, b, (((1,), (0,)), ((), ())), precision=precision, preferred_element_type=jnp.float32
    )


def split(a):
    high = a.astype(jnp.bfloat16)
    return high, (a - high.astype(jnp.float32)).astype(jnp.bfloat16)


def three(dot, a, b):
    (ah, al), (bh, bl) = a, b
    return dot(ah, bh, None) + (dot(ah, bl, None) + dot(al, bh, None))


def comm_kernel(
    ranks, x_hbm, cot_hbm, fb_hbm, q_hbm,
    g_out, s_out, p_out, r_out, li_out,
    xb, ct, fb, qv, gx, cf_h, cf_l, pp, pq, pr, rs, pf3, pf_x, s_src, s_rs, s_t, s_z, gl, g_rs, gg, mat,
    l_sem, pr_send, pr_recv, a_send, a_recv, b_send, b_recv, z_send, z_recv, f_send, f_recv, near,
):
    z, c, x, y = (lax.axis_index(n) for n in ("z", "c", "x", "y"))
    oc = 1 - c
    f = x * NY + y
    pending = []

    def at(dz=0, dx=0, dy=0):
        return (lax.rem(z + dz, NZ), c, lax.rem(x + dx, NX), lax.rem(y + dy, NY))

    partner = (z, oc, x, y)

    def send(src, dst, ssem, rsem, dev):
        cp = pltpu.make_async_remote_copy(
            src_ref=src, dst_ref=dst, send_sem=ssem, recv_sem=rsem, device_id=dev, device_id_type=MESH
        )
        cp.start()
        pending.append(cp)

    def arrive(dst, ssem, rsem, dev):
        pltpu.make_async_remote_copy(
            src_ref=dst, dst_ref=dst, send_sem=ssem, recv_sem=rsem, device_id=dev, device_id_type=MESH
        ).wait_recv()

    barrier = pltpu.get_barrier_semaphore()
    peers = [partner] + [at(dx=dx) for dx in (1, 2, 3)]
    peers += [at(dy=1), at(dy=NY - 1), at(dz=1), at(dz=NZ - 1)]
    for peer in peers:
        pl.semaphore_signal(barrier, inc=1, device_id=peer, device_id_type=MESH)

    loads = [
        pltpu.make_async_copy(src, dst, l_sem.at[i])
        for i, (src, dst) in enumerate(
            [(cot_hbm.at[r], ct.at[r, x, y]) for r in range(2)] + [(x_hbm, xb), (fb_hbm, fb), (q_hbm, qv)]
        )
    ]
    for cp in loads:
        cp.start()
    for cp in loads[:2]:
        cp.wait()

    pl.semaphore_wait(barrier, len(peers))

    def tell(r):
        for n, dz in enumerate((1, NZ - 1)):
            pl.semaphore_signal(near.at[r - 1, n], inc=1, device_id=at(dz=dz), device_id_type=MESH)

    def told(r):
        for n in range(2):
            pl.semaphore_wait(near.at[r - 1, n], 1)

    def chunk(r, dx, dy):
        return ct.at[r, lax.rem(x + dx + NX, NX), lax.rem(y + dy + NY, NY)]

    def a_y(dirn, s):
        k = chunk(0, 0, -dirn * (s - 1))
        i = (s - 1) if dirn > 0 else 3 + s
        send(k, k, a_send.at[i], a_recv.at[i], at(dy=dirn % NY))

    def a_y_wait(dirn, s):
        i = (s - 1) if dirn > 0 else 3 + s
        arrive(chunk(0, 0, -dirn * s), a_send.at[i], a_recv.at[i], at(dy=-dirn % NY))

    def a_x(j, dirn):
        k = chunk(0, 0, -j)
        i = 8 + j * 3 + (0 if dirn > 0 else 1)
        send(k, k, a_send.at[i], a_recv.at[i], at(dx=dirn % NX))

    def a_x_wait(j, dirn):
        i = 8 + j * 3 + (0 if dirn > 0 else 1)
        arrive(chunk(0, -dirn, -j), a_send.at[i], a_recv.at[i], at(dx=-dirn % NX))

    def far_dir(j):
        return 1 if j % 2 == 0 else -1

    def a_x_far(j):
        d = far_dir(j)
        k = chunk(0, -d, -j)
        i = 8 + j * 3 + 2
        send(k, k, a_send.at[i], a_recv.at[i], at(dx=d % NX))

    def a_x_far_wait(j):
        d = far_dir(j)
        i = 8 + j * 3 + 2
        arrive(chunk(0, -2 * d, -j), a_send.at[i], a_recv.at[i], at(dx=-d % NX))

    def b_x(dx):
        k = chunk(1, 0, 0)
        send(k, k, b_send.at[dx], b_recv.at[dx], at(dx=dx))

    def b_x_wait(dx):
        arrive(chunk(1, -dx, 0), b_send.at[dx], b_recv.at[dx], at(dx=NX - dx))

    def b_reach(dx, dirn):
        return (4 if dirn > 0 else 3) if dx % 2 == 0 else (3 if dirn > 0 else 4)

    def b_idx(dx, dirn, s):
        return 4 + dx * 8 + (s - 1 if dirn > 0 else 3 + s)

    def b_y(dx, dirn, s):
        k = chunk(1, -dx, -dirn * (s - 1))
        i = b_idx(dx, dirn, s)
        send(k, k, b_send.at[i], b_recv.at[i], at(dy=dirn % NY))

    def b_y_wait(dx, dirn, s):
        i = b_idx(dx, dirn, s)
        arrive(chunk(1, -dx, -dirn * s), b_send.at[i], b_recv.at[i], at(dy=-dirn % NY))

    a_y(1, 1)
    a_y(-1, 1)
    a_x(0, 1)
    a_x(0, -1)

    for dx in (1, 3, 2):
        b_x(dx)
    b_y(0, 1, 1)
    b_y(0, -1, 1)
    tell(1)

    for s in range(1, 5):
        a_y_wait(1, s)
        if s < 4:
            a_y(1, s + 1)
        a_x(s, 1)
        a_x(s, -1)
        if s < 4:
            a_y_wait(-1, s)
            if s < 3:
                a_y(-1, s + 1)
            a_x(NY - s, 1)
            a_x(NY - s, -1)
        if s == 1:
            for dx in (1, 3, 2):
                b_x_wait(dx)
                b_y(dx, 1, 1)
                b_y(dx, -1, 1)
        for dx in (0, 1, 3, 2):
            for dirn in (1, -1):
                if s <= b_reach(dx, dirn):
                    b_y_wait(dx, dirn, s)
                    if s < b_reach(dx, dirn):
                        b_y(dx, dirn, s + 1)
        told(s)
        tell(s + 1)
        ready = {1: (0,), 2: (1, 7), 3: (2, 6), 4: (3, 5)}[s]
        for j in ready:
            d = far_dir(j)
            a_x_wait(j, d)
            a_x_far(j)
            a_x_wait(j, -d)
    d = far_dir(4)
    a_x_wait(4, d)
    a_x_far(4)
    a_x_wait(4, -d)
    told(5)
    for cp in loads[2:]:
        cp.wait()
    x_t = xb[...].astype(jnp.float32).T.astype(jnp.bfloat16)
    for j in (0, 1, 7, 2, 6, 3, 5, 4):
        a_x_far_wait(j)

    width = lax.broadcasted_iota(jnp.int32, (1, 128), 1)
    rank = ranks[c]
    for m, out in ((oc, pq), (c, pp)):
        live = width < ranks[m]
        total = jnp.zeros((256, 128), jnp.float32)
        for b in range(NX):
            cols = pl.ds(b * 256, 256)
            full = fb[m, 0, :, cols] + nt(x_t, ct[m, b].reshape(256, 512), None)
            g_out[m, :, cols] = full
            total = total + three(nn, split(full), split(jnp.where(live, qv[m, cols, :], 0.0)))
        for i in range(NZ):
            lo, hi = i * PIECE, min((i + 1) * PIECE, 256)
            if hi - lo == PIECE:
                out[i] = total[lo:hi]
            elif hi > lo:
                out[i, : hi - lo] = total[lo:hi]
                out[i, hi - lo :] = jnp.zeros((PIECE - (hi - lo), 128), jnp.float32)
            else:
                out[i] = jnp.zeros((PIECE, 128), jnp.float32)
        if out is pq:
            send(pq, pr, pr_send.at[0], pr_recv.at[0], partner)
    arrive(pr, pr_send.at[0], pr_recv.at[0], partner)
    pp[...] = pp[...] + pr[...]

    for d in ZOFFS:
        send(pp.at[lax.rem(z + d, NZ)], rs.at[d], z_send.at[d], z_recv.at[d], at(dz=d))
    for b in range(4):
        rows = pl.ds(b * 64, 64)
        send(g_out.at[oc, rows], gx.at[rows], pr_send.at[1 + b], pr_recv.at[1 + b], partner)
    acc = pp[z]
    for d in reversed(ZOFFS):
        arrive(rs.at[d], z_send.at[d], z_recv.at[d], at(dz=NZ - d))
        acc = acc + rs[d]
    pf3[z] = acc
    for d in ZOFFS:
        send(pf3.at[z], pf3.at[z], z_send.at[12 + d], z_recv.at[12 + d], at(dz=d))
    for b in range(4):
        rows = pl.ds(b * 64, 64)
        arrive(gx.at[rows], pr_send.at[1 + b], pr_recv.at[1 + b], partner)
    for b in range(NX):
        cols = pl.ds(b * 256, 256)
        cf_h[cols, :], cf_l[cols, :] = split((g_out[c, :, cols] + gx[:, cols]).T)
    for d in reversed(ZOFFS):
        zs = lax.rem(z + NZ - d, NZ)
        arrive(pf3.at[zs], z_send.at[12 + d], z_recv.at[12 + d], at(dz=NZ - d))
    left = pf3[...].reshape(NZ * PIECE, 128)[:256]

    gram = nn(left.T, left)
    for i in range(NF):
        gl[i] = gram[4 * i : 4 * i + 4]
    for n, (dx, dy) in enumerate(OFFS):
        to = lax.rem(x + dx, NX) * NY + lax.rem(y + dy, NY)
        send(gl.at[to], g_rs.at[n], f_send.at[n], f_recv.at[n], at(dx=dx, dy=dy))
    left_parts = split(left)
    for b in range(NX):
        rows = pl.ds(b * 256, 256)
        s_src[pl.ds(b * NY, NY)] = three(nn, (cf_h[rows, :], cf_l[rows, :]), left_parts).reshape(NY, 32, 128)
    for dy in YOFFS + (0,):
        for dx in (2, 1, 3):
            to = lax.rem(x + dx, NX) * NY + lax.rem(y + dy, NY)
            i = dx * NY + dy
            send(s_src.at[to], s_rs.at[i], f_send.at[32 + i], f_recv.at[32 + i], at(dx=dx))

    send(pf3, pf_x, pr_send.at[5], pr_recv.at[5], partner)

    def src(dx, dy):
        return at(dx=(NX - dx) % NX, dy=(NY - dy) % NY)

    def gram_owner():
        acc = gl[f]
        for n, (dx, dy) in reversed(list(enumerate(OFFS))):
            arrive(g_rs.at[n], f_send.at[n], f_recv.at[n], src(dx, dy))
            acc = acc + g_rs[n]
        gg[f] = acc
        for n, (dx, dy) in enumerate(OFFS):
            send(gg.at[f], gg.at[f], f_send.at[64 + n], f_recv.at[64 + n], at(dx=dx, dy=dy))

    for dy in YOFFS + (0,):
        if dy == 2:
            gram_owner()
        acc = s_src[x * NY + lax.rem(y + dy, NY)]
        for dx in (1, 3, 2):
            i = dx * NY + dy
            arrive(s_rs.at[i], f_send.at[32 + i], f_recv.at[32 + i], at(dx=NX - dx))
            acc = acc + s_rs[i]
        if dy:
            s_t[dy] = acc
            send(s_t.at[dy], s_rs.at[dy], f_send.at[32 + dy], f_recv.at[32 + dy], at(dy=dy))
    for dy in reversed(YOFFS):
        arrive(s_rs.at[dy], f_send.at[32 + dy], f_recv.at[32 + dy], at(dy=NY - dy))
        acc = acc + s_rs[dy]
    s_z[z] = acc
    for d in ZOFFS:
        send(s_z.at[z], s_z.at[z], z_send.at[24 + d], z_recv.at[24 + d], at(dz=d))

    for n, (dx, dy) in reversed(list(enumerate(OFFS))):
        sx, sy = lax.rem(x + NX - dx, NX), lax.rem(y + NY - dy, NY)
        arrive(gg.at[sx * NY + sy], f_send.at[64 + n], f_recv.at[64 + n], src(dx, dy))
    for i in range(NF):
        mat[4 * i : 4 * i + 4, :] = gg[i]
    row_id = lax.broadcasted_iota(jnp.int32, (128, 128), 0)
    col_id = lax.broadcasted_iota(jnp.int32, (128, 128), 1)
    mat[...] = mat[...] + jnp.where((row_id == col_id) & (col_id >= rank), 1.0, 0.0)

    def eliminate(j, carry):
        m = mat[...]
        row = mat[pl.ds(j, 1), :]
        hit = col_id == j
        hit1 = width == j
        pivot = jnp.sum(jnp.where(hit1, row, 0.0), axis=1, keepdims=True)
        col = jnp.sum(jnp.where(hit, m, 0.0), axis=1, keepdims=True)
        factor = jnp.where(row_id > j, col / pivot, 0.0)
        mat[...] = jnp.where(hit & (row_id > j), 0.0, m) - factor * jnp.where(hit1, 1.0, row)
        return carry

    lax.fori_loop(0, STEPS[0], eliminate, 0)

    for d in reversed(ZOFFS):
        zs = lax.rem(z + NZ - d, NZ)
        arrive(s_z.at[zs], z_send.at[24 + d], z_recv.at[24 + d], at(dz=NZ - d))
    acc = s_z[0]
    for i in range(1, NZ):
        acc = acc + s_z[i]
    s_out[c, f] = acc

    def piece(dx, dy):
        return lax.rem(x + NX - dx, NX) * NY + lax.rem(y + NY - dy, NY)

    def forward(dx, dy):
        k, i = piece(dx, dy), 128 + dx * NY + dy
        send(s_out.at[c, k], s_out.at[c, k], f_send.at[i], f_recv.at[i], partner)

    def spread(dy):
        k = piece(0, dy)
        for dx in (2, 1, 3):
            i = 96 + dx * NY + dy
            send(s_out.at[c, k], s_out.at[c, k], f_send.at[i], f_recv.at[i], at(dx=dx))
        forward(0, dy)

    for dy in YOFFS:
        send(s_out.at[c, f], s_out.at[c, f], f_send.at[96 + dy], f_recv.at[96 + dy], at(dy=dy))
    spread(0)
    lax.fori_loop(STEPS[0], STEPS[1], eliminate, 0)
    for dy in reversed(YOFFS):
        arrive(s_out.at[c, piece(0, dy)], f_send.at[96 + dy], f_recv.at[96 + dy], at(dy=NY - dy))
        spread(dy)

    lax.fori_loop(STEPS[1], 128, eliminate, 0)
    m = mat[...]
    diag = jnp.sum(jnp.where(row_id == col_id, m, 0.0), axis=1, keepdims=True)
    unit = jnp.where(row_id == col_id, 1.0, jnp.where(row_id > col_id, m, 0.0))
    li_out[c] = unit * (1.0 / jnp.sqrt(diag))
    send(li_out.at[c], li_out.at[c], pr_send.at[6], pr_recv.at[6], partner)

    def factor(m, parts):
        inv = split(li_out[m])
        own = three(nt, parts, inv)
        p_out[m] = own
        r_out[m] = three(nn, split(own), inv)

    factor(c, left_parts)
    for dy in (0,) + YOFFS[::-1]:
        for dx in (1, 3, 2):
            i = 96 + dx * NY + dy
            arrive(s_out.at[c, piece(dx, dy)], f_send.at[i], f_recv.at[i], at(dx=NX - dx))
            forward(dx, dy)
    arrive(pf_x, pr_send.at[5], pr_recv.at[5], partner)
    arrive(li_out.at[oc], pr_send.at[6], pr_recv.at[6], partner)
    factor(oc, split(pf_x[...].reshape(NZ * PIECE, 128)[:256]))
    for dy in (0,) + YOFFS[::-1]:
        for dx in range(NX):
            i = 128 + dx * NY + dy
            arrive(s_out.at[oc, piece(dx, dy)], f_send.at[i], f_recv.at[i], partner)
    for cp in pending:
        cp.wait_send()


def final_kernel(g, s, p, r, li, p_out, q_out, e_out, q_buf, e_buf, sem):
    puts = []

    def put(src, dst):
        puts.append(pltpu.make_async_copy(src, dst, sem.at[len(puts)]))
        puts[-1].start()

    put(p, p_out)
    for m in range(2):
        inv, right = split(li[m]), split(r[m])
        for b in range(NX):
            cols = pl.ds(b * 256, 256)
            raw = split(s[m, b * NY : (b + 1) * NY].reshape(256, 128))
            e_buf[m, :, cols] = g[m, :, cols] - three(nt, right, raw)
            put(e_buf.at[m, :, cols], e_out.at[m, 0, :, cols])
            q_buf[m, cols, :] = three(nt, raw, inv)
            put(q_buf.at[m, cols, :], q_out.at[m, cols, :])
    for cp in puts:
        cp.wait()


def local(inputs, cotangent, feedback, q_init, factor_ranks):
    f32, b16 = jnp.float32, jnp.bfloat16
    vm = pl.BlockSpec(memory_space=pltpu.VMEM)
    anyspace = pl.BlockSpec(memory_space=pl.ANY)
    dma = pltpu.SemaphoreType.DMA
    parts = pl.pallas_call(
        comm_kernel,
        out_shape=(
            pltpu.VMEM((2, 256, 1024), f32),
            pltpu.VMEM((2, NF, 32, 128), f32),
            pltpu.VMEM((2, 256, 128), f32),
            pltpu.VMEM((2, 256, 128), f32),
            pltpu.VMEM((2, 128, 128), f32),
        ),
        in_specs=[pl.BlockSpec(memory_space=pltpu.SMEM)] + [anyspace] * 4,
        out_specs=(vm,) * 5,
        scratch_shapes=[
            pltpu.VMEM((512, 256), b16),
            pltpu.VMEM((2, NX, NY, 32, 512), b16),
            pltpu.VMEM((2, 1, 256, 1024), f32),
            pltpu.VMEM((2, 1024, 128), f32),
            pltpu.VMEM((256, 1024), f32),
            pltpu.VMEM((1024, 256), b16),
            pltpu.VMEM((1024, 256), b16),
            pltpu.VMEM((NZ, PIECE, 128), f32),
            pltpu.VMEM((NZ, PIECE, 128), f32),
            pltpu.VMEM((NZ, PIECE, 128), f32),
            pltpu.VMEM((NZ, PIECE, 128), f32),
            pltpu.VMEM((NZ, PIECE, 128), f32),
            pltpu.VMEM((NZ, PIECE, 128), f32),
            pltpu.VMEM((NF, 32, 128), f32),
            pltpu.VMEM((NF, 32, 128), f32),
            pltpu.VMEM((NY, 32, 128), f32),
            pltpu.VMEM((NZ, 32, 128), f32),
            pltpu.VMEM((NF, 4, 128), f32),
            pltpu.VMEM((NF, 4, 128), f32),
            pltpu.VMEM((NF, 4, 128), f32),
            pltpu.VMEM((128, 128), f32),
            dma((5,)),
            dma((7,)), dma((7,)),
            dma((32,)), dma((32,)),
            dma((36,)), dma((36,)),
            dma((36,)), dma((36,)),
            dma((160,)), dma((160,)),
            pltpu.SemaphoreType.REGULAR((5, 2)),
        ],
        compiler_params=pltpu.CompilerParams(
            collective_id=0, has_side_effects=True, vmem_limit_bytes=32 << 20
        ),
        name="exchange",
    )(factor_ranks, inputs, jnp.swapaxes(cotangent, 1, 2), feedback, q_init)
    return pl.pallas_call(
        final_kernel,
        out_shape=(
            jax.ShapeDtypeStruct((2, 256, 128), f32),
            jax.ShapeDtypeStruct((2, 1024, 128), f32),
            jax.ShapeDtypeStruct((2, 1, 256, 1024), f32),
        ),
        in_specs=[vm] * 5,
        out_specs=(anyspace,) * 3,
        scratch_shapes=[pltpu.VMEM((2, 1024, 128), f32), pltpu.VMEM((2, 256, 1024), f32), dma((17,))],
        compiler_params=pltpu.CompilerParams(vmem_limit_bytes=16 << 20),
        name="finish",
    )(*parts)


def solution(mesh):
    torus = Mesh(mesh.devices.reshape(NZ, 2, NX, NY), ("z", "c", "x", "y"))
    placed = (P(DP, FS), P(None, DP, FS), P(None, DP, FS, None), P(), P())
    return jax.shard_map(
        local,
        mesh=torus,
        in_specs=placed,
        out_specs=(P(None, FS, None), P(), P(None, DP, FS, None)),
        check_vma=False,
    )
```

```python
import functools

import jax
import jax.numpy as jnp
from jax import lax
from jax.experimental import pallas as pl
from jax.experimental.pallas import tpu as pltpu
from jax.sharding import Mesh
from jax.sharding import PartitionSpec as P

MESH = pl.DeviceIdType.MESH
HI = lax.Precision.HIGHEST
NZ, NX, NY = 12, 4, 8
NF = NX * NY
STEPS = (48, 80)
PIECE = 24
DP = ("z", "c")
FS = ("x", "y")

OFFS = sorted(
    [(dx, dy) for dx in range(NX) for dy in range(NY) if dx or dy],
    key=lambda o: -(min(o[0], NX - o[0]) + min(o[1], NY - o[1])),
)
YOFFS = (4, 3, 5, 2, 6, 1, 7)
ZOFFS = sorted(range(1, NZ), key=lambda d: -min(d, NZ - d))


def nt(a, b, precision=HI):
    return lax.dot_general(
        a, b, (((1,), (1,)), ((), ())), precision=precision, preferred_element_type=jnp.float32
    )


def nn(a, b, precision=HI):
    return lax.dot_general(
        a, b, (((1,), (0,)), ((), ())), precision=precision, preferred_element_type=jnp.float32
    )


def split(a):
    high = a.astype(jnp.bfloat16)
    return high, (a - high.astype(jnp.float32)).astype(jnp.bfloat16)


def three(dot, a, b):
    (ah, al), (bh, bl) = a, b
    return dot(ah, bh, None) + (dot(ah, bl, None) + dot(al, bh, None))


def comm_kernel(
    ranks, x_hbm, cot_hbm, fb_hbm, q_hbm,
    g_out, s_out, p_out, r_out, li_out,
    xb, ct, fb, qv, gx, cf_h, cf_l, pp, pq, pr, rs, pf3, pf_x, s_src, s_rs, s_t, s_z, gl, g_rs, gg, mat,
    l_sem, pr_send, pr_recv, a_send, a_recv, b_send, b_recv, z_send, z_recv, f_send, f_recv, near,
):
    z, c, x, y = (lax.axis_index(n) for n in ("z", "c", "x", "y"))
    oc = 1 - c
    f = x * NY + y
    pending = []

    def at(dz=0, dx=0, dy=0):
        return (lax.rem(z + dz, NZ), c, lax.rem(x + dx, NX), lax.rem(y + dy, NY))

    partner = (z, oc, x, y)

    def send(src, dst, ssem, rsem, dev):
        cp = pltpu.make_async_remote_copy(
            src_ref=src, dst_ref=dst, send_sem=ssem, recv_sem=rsem, device_id=dev, device_id_type=MESH
        )
        cp.start()
        pending.append(cp)

    def settle(count=None):
        for cp in pending[:count]:
            cp.wait_send()
        del pending[:count]

    def batch(src, dst, sems, k, dev):
        pltpu.make_async_remote_copy(
            src_ref=src, dst_ref=dst, send_sem=sems[0].at[k], recv_sem=sems[1].at[k], device_id=dev, device_id_type=MESH
        ).start()

    def whole(ref, sems, k):
        return pltpu.make_async_remote_copy(
            src_ref=ref, dst_ref=ref, send_sem=sems[0].at[k], recv_sem=sems[1].at[k],
            device_id=partner, device_id_type=MESH,
        )

    def arrive(dst, ssem, rsem, dev):
        pltpu.make_async_remote_copy(
            src_ref=dst, dst_ref=dst, send_sem=ssem, recv_sem=rsem, device_id=dev, device_id_type=MESH
        ).wait_recv()

    barrier = pltpu.get_barrier_semaphore()
    peers = [partner] + [at(dx=dx) for dx in (1, 2, 3)]
    peers += [at(dy=1), at(dy=NY - 1), at(dz=1), at(dz=NZ - 1)]
    for peer in peers:
        pl.semaphore_signal(barrier, inc=1, device_id=peer, device_id_type=MESH)

    loads = [
        pltpu.make_async_copy(src, dst, l_sem.at[i])
        for i, (src, dst) in enumerate(
            [(cot_hbm.at[r], ct.at[r, x, y]) for r in range(2)] + [(x_hbm, xb), (fb_hbm, fb), (q_hbm, qv)]
        )
    ]
    for cp in loads:
        cp.start()
    for cp in loads[:2]:
        cp.wait()

    pl.semaphore_wait(barrier, len(peers))

    def tell(r):
        for n, dz in enumerate((1, NZ - 1)):
            pl.semaphore_signal(near.at[r - 1, n], inc=1, device_id=at(dz=dz), device_id_type=MESH)

    def told(r):
        for n in range(2):
            pl.semaphore_wait(near.at[r - 1, n], 1)

    def chunk(r, dx, dy):
        return ct.at[r, lax.rem(x + dx + NX, NX), lax.rem(y + dy + NY, NY)]

    def a_y(dirn, s):
        k = chunk(0, 0, -dirn * (s - 1))
        i = (s - 1) if dirn > 0 else 3 + s
        send(k, k, a_send.at[i], a_recv.at[i], at(dy=dirn % NY))

    def a_y_wait(dirn, s):
        i = (s - 1) if dirn > 0 else 3 + s
        arrive(chunk(0, 0, -dirn * s), a_send.at[i], a_recv.at[i], at(dy=-dirn % NY))

    def a_x(j, dirn):
        k = chunk(0, 0, -j)
        i = 8 + j * 3 + (0 if dirn > 0 else 1)
        send(k, k, a_send.at[i], a_recv.at[i], at(dx=dirn % NX))

    def a_x_wait(j, dirn):
        i = 8 + j * 3 + (0 if dirn > 0 else 1)
        arrive(chunk(0, -dirn, -j), a_send.at[i], a_recv.at[i], at(dx=-dirn % NX))

    def far_dir(j):
        return 1 if j % 2 == 0 else -1

    def a_x_far(j):
        d = far_dir(j)
        k = chunk(0, -d, -j)
        i = 8 + j * 3 + 2
        send(k, k, a_send.at[i], a_recv.at[i], at(dx=d % NX))

    def a_x_far_wait(j):
        d = far_dir(j)
        i = 8 + j * 3 + 2
        arrive(chunk(0, -2 * d, -j), a_send.at[i], a_recv.at[i], at(dx=-d % NX))

    def b_x(dx):
        k = chunk(1, 0, 0)
        send(k, k, b_send.at[dx], b_recv.at[dx], at(dx=dx))

    def b_x_wait(dx):
        arrive(chunk(1, -dx, 0), b_send.at[dx], b_recv.at[dx], at(dx=NX - dx))

    def b_reach(dx, dirn):
        return (4 if dirn > 0 else 3) if dx % 2 == 0 else (3 if dirn > 0 else 4)

    def b_idx(dx, dirn, s):
        return 4 + dx * 8 + (s - 1 if dirn > 0 else 3 + s)

    def b_y(dx, dirn, s):
        k = chunk(1, -dx, -dirn * (s - 1))
        i = b_idx(dx, dirn, s)
        send(k, k, b_send.at[i], b_recv.at[i], at(dy=dirn % NY))

    def b_y_wait(dx, dirn, s):
        i = b_idx(dx, dirn, s)
        arrive(chunk(1, -dx, -dirn * s), b_send.at[i], b_recv.at[i], at(dy=-dirn % NY))

    a_y(1, 1)
    a_y(-1, 1)
    a_x(0, 1)
    a_x(0, -1)

    for dx in (1, 3, 2):
        b_x(dx)
    b_y(0, 1, 1)
    b_y(0, -1, 1)
    tell(1)

    def a_hop(s):
        for dirn, last in ((1, 4), (-1, 3)):
            if s <= last:
                a_y_wait(dirn, s)
                if s < last:
                    a_y(dirn, s + 1)
        for j in (s, NY - s) if s < 4 else (4,):
            a_x(j, 1)
            a_x(j, -1)

    def a_far(j):
        d = far_dir(j)
        a_x_wait(j, d)
        a_x_far(j)
        a_x_wait(j, -d)

    def b_hop(s, dxs):
        for dx in dxs:
            for dirn in (1, -1):
                if s <= b_reach(dx, dirn):
                    b_y_wait(dx, dirn, s)
                    if s < b_reach(dx, dirn):
                        b_y(dx, dirn, s + 1)

    a_hop(1)
    for dx in (1, 3, 2):
        b_x_wait(dx)
        b_y(dx, 1, 1)
        b_y(dx, -1, 1)
    for s in range(1, 5):
        b_hop(s, (0,))
        told(s)
        tell(s + 1)
        if s < 4:
            a_hop(s + 1)
        b_hop(s, (1, 3, 2))
        for j in {1: (0,), 2: (1, 7), 3: (2, 6), 4: (3, 5, 4)}[s]:
            a_far(j)
    told(5)
    for cp in loads[2:]:
        cp.wait()
    x_t = xb[...].astype(jnp.float32).T.astype(jnp.bfloat16)
    for j in (0, 1, 7, 2, 6, 3, 5, 4):
        a_x_far_wait(j)

    width = lax.broadcasted_iota(jnp.int32, (1, 128), 1)
    rank = ranks[c]
    for m, out in ((oc, pq), (c, pp)):
        live = width < ranks[m]
        total = jnp.zeros((256, 128), jnp.float32)
        for b in range(NX):
            cols = pl.ds(b * 256, 256)
            full = fb[m, 0, :, cols] + nt(x_t, ct[m, b].reshape(256, 512), None)
            g_out[m, :, cols] = full
            total = total + three(nn, split(full), split(jnp.where(live, qv[m, cols, :], 0.0)))
        for i in range(NZ):
            lo, hi = i * PIECE, min((i + 1) * PIECE, 256)
            if hi - lo == PIECE:
                out[i] = total[lo:hi]
            elif hi > lo:
                out[i, : hi - lo] = total[lo:hi]
                out[i, hi - lo :] = jnp.zeros((PIECE - (hi - lo), 128), jnp.float32)
            else:
                out[i] = jnp.zeros((PIECE, 128), jnp.float32)
        if out is pq:
            send(pq, pr, pr_send.at[0], pr_recv.at[0], partner)
    arrive(pr, pr_send.at[0], pr_recv.at[0], partner)
    pp[...] = pp[...] + pr[...]

    sent = len(pending)
    zs_sems = (z_send, z_recv)
    for d in ZOFFS:
        batch(pp.at[lax.rem(z + d, NZ)], rs.at[d], zs_sems, 0, at(dz=d))
    for b in range(4):
        rows = pl.ds(b * 64, 64)
        send(g_out.at[oc, rows], gx.at[rows], pr_send.at[1 + b], pr_recv.at[1 + b], partner)
    settle(sent)
    pieces = whole(rs.at[pl.ds(1, NZ - 1)], zs_sems, 0)
    pieces.wait_recv()
    acc = pp[z]
    for d in range(1, NZ):
        acc = acc + rs[d]
    pf3[z] = acc
    for d in ZOFFS:
        batch(pf3.at[z], pf3.at[z], zs_sems, 1, at(dz=d))
    pieces.wait_send()
    for b in range(4):
        rows = pl.ds(b * 64, 64)
        arrive(gx.at[rows], pr_send.at[1 + b], pr_recv.at[1 + b], partner)
    for b in range(NX):
        cols = pl.ds(b * 256, 256)
        cf_h[cols, :], cf_l[cols, :] = split((g_out[c, :, cols] + gx[:, cols]).T)
    settle()
    pieces = whole(pf3.at[pl.ds(0, NZ - 1)], zs_sems, 1)
    pieces.wait_recv()
    pieces.wait_send()
    left = pf3[...].reshape(NZ * PIECE, 128)[:256]

    f_sems = (f_send, f_recv)
    gram = nn(left.T, left)
    for i in range(NF):
        gl[i] = gram[4 * i : 4 * i + 4]
    for n, (dx, dy) in enumerate(OFFS):
        to = lax.rem(x + dx, NX) * NY + lax.rem(y + dy, NY)
        batch(gl.at[to], g_rs.at[n], f_sems, 0, at(dx=dx, dy=dy))
    left_parts = split(left)
    for b in range(NX):
        rows = pl.ds(b * 256, 256)
        s_src[pl.ds(b * NY, NY)] = three(nn, (cf_h[rows, :], cf_l[rows, :]), left_parts).reshape(NY, 32, 128)
    for dy in YOFFS + (0,):
        for dx in (2, 1, 3):
            to = lax.rem(x + dx, NX) * NY + lax.rem(y + dy, NY)
            i = dx * NY + dy
            send(s_src.at[to], s_rs.at[i], f_send.at[32 + i], f_recv.at[32 + i], at(dx=dx))

    send(pf3, pf_x, pr_send.at[5], pr_recv.at[5], partner)

    def gram_owner():
        pieces = whole(g_rs.at[pl.ds(0, NF - 1)], f_sems, 0)
        pieces.wait_recv()
        acc = gl[f]
        for n in range(NF - 1):
            acc = acc + g_rs[n]
        gg[f] = acc
        for dx, dy in OFFS:
            batch(gg.at[f], gg.at[f], f_sems, 1, at(dx=dx, dy=dy))
        pieces.wait_send()

    for dy in YOFFS + (0,):
        if dy == 2:
            gram_owner()
        acc = s_src[x * NY + lax.rem(y + dy, NY)]
        for dx in (1, 3, 2):
            i = dx * NY + dy
            arrive(s_rs.at[i], f_send.at[32 + i], f_recv.at[32 + i], at(dx=NX - dx))
            acc = acc + s_rs[i]
        if dy:
            s_t[dy] = acc
            batch(s_t.at[dy], s_rs.at[dy], f_sems, 2, at(dy=dy))
    settle()
    pieces = whole(s_rs.at[pl.ds(1, NY - 1)], f_sems, 2)
    pieces.wait_recv()
    for dy in range(1, NY):
        acc = acc + s_rs[dy]
    s_z[z] = acc
    for d in ZOFFS:
        batch(s_z.at[z], s_z.at[z], zs_sems, 2, at(dz=d))
    pieces.wait_send()

    pieces = whole(gg.at[pl.ds(0, NF - 1)], f_sems, 1)
    pieces.wait_recv()
    pieces.wait_send()
    for i in range(NF):
        mat[4 * i : 4 * i + 4, :] = gg[i]
    row_id = lax.broadcasted_iota(jnp.int32, (128, 128), 0)
    col_id = lax.broadcasted_iota(jnp.int32, (128, 128), 1)
    mat[...] = mat[...] + jnp.where((row_id == col_id) & (col_id >= rank), 1.0, 0.0)

    def eliminate(j, carry):
        m = mat[...]
        row = mat[pl.ds(j, 1), :]
        hit = col_id == j
        hit1 = width == j
        pivot = jnp.sum(jnp.where(hit1, row, 0.0), axis=1, keepdims=True)
        col = jnp.sum(jnp.where(hit, m, 0.0), axis=1, keepdims=True)
        factor = jnp.where(row_id > j, col / pivot, 0.0)
        mat[...] = jnp.where(hit & (row_id > j), 0.0, m) - factor * jnp.where(hit1, 1.0, row)
        return carry

    lax.fori_loop(0, STEPS[0], eliminate, 0)

    pieces = whole(s_z.at[pl.ds(0, NZ - 1)], zs_sems, 2)
    pieces.wait_recv()
    pieces.wait_send()
    acc = s_z[0]
    for i in range(1, NZ):
        acc = acc + s_z[i]
    s_out[c, f] = acc

    def piece(dx, dy):
        return lax.rem(x + NX - dx, NX) * NY + lax.rem(y + NY - dy, NY)

    def forward(dx, dy):
        k = piece(dx, dy)
        batch(s_out.at[c, k], s_out.at[c, k], f_sems, 3, partner)

    def spread(dy):
        k = piece(0, dy)
        for dx in (2, 1, 3):
            i = 96 + dx * NY + dy
            send(s_out.at[c, k], s_out.at[c, k], f_send.at[i], f_recv.at[i], at(dx=dx))
        forward(0, dy)

    for dy in YOFFS:
        send(s_out.at[c, f], s_out.at[c, f], f_send.at[96 + dy], f_recv.at[96 + dy], at(dy=dy))
    spread(0)
    lax.fori_loop(STEPS[0], STEPS[1], eliminate, 0)
    for dy in reversed(YOFFS):
        arrive(s_out.at[c, piece(0, dy)], f_send.at[96 + dy], f_recv.at[96 + dy], at(dy=NY - dy))
        spread(dy)

    lax.fori_loop(STEPS[1], 128, eliminate, 0)
    m = mat[...]
    diag = jnp.sum(jnp.where(row_id == col_id, m, 0.0), axis=1, keepdims=True)
    unit = jnp.where(row_id == col_id, 1.0, jnp.where(row_id > col_id, m, 0.0))
    li_out[c] = unit * (1.0 / jnp.sqrt(diag))
    send(li_out.at[c], li_out.at[c], pr_send.at[6], pr_recv.at[6], partner)

    def factor(m, parts):
        inv = split(li_out[m])
        own = three(nt, parts, inv)
        p_out[m] = own
        r_out[m] = three(nn, split(own), inv)

    factor(c, left_parts)
    settle()
    for dy in (0,) + YOFFS[::-1]:
        for dx in (1, 3, 2):
            i = 96 + dx * NY + dy
            arrive(s_out.at[c, piece(dx, dy)], f_send.at[i], f_recv.at[i], at(dx=NX - dx))
            forward(dx, dy)
    arrive(pf_x, pr_send.at[5], pr_recv.at[5], partner)
    arrive(li_out.at[oc], pr_send.at[6], pr_recv.at[6], partner)
    factor(oc, split(pf_x[...].reshape(NZ * PIECE, 128)[:256]))
    pieces = whole(s_out.at[oc], f_sems, 3)
    pieces.wait_recv()
    pieces.wait_send()


def final_kernel(g, s, p, r, li, p_out, q_out, e_out, q_buf, e_buf, sem):
    puts = []

    def put(src, dst):
        puts.append(pltpu.make_async_copy(src, dst, sem.at[len(puts)]))
        puts[-1].start()

    put(p, p_out)
    for m in range(2):
        inv, right = split(li[m]), split(r[m])
        for b in range(NX):
            cols = pl.ds(b * 256, 256)
            raw = split(s[m, b * NY : (b + 1) * NY].reshape(256, 128))
            e_buf[m, :, cols] = g[m, :, cols] - three(nt, right, raw)
            put(e_buf.at[m, :, cols], e_out.at[m, 0, :, cols])
            q_buf[m, cols, :] = three(nt, raw, inv)
            put(q_buf.at[m, cols, :], q_out.at[m, cols, :])
    for cp in puts:
        cp.wait()


def local(inputs, cotangent, feedback, q_init, factor_ranks):
    f32, b16 = jnp.float32, jnp.bfloat16
    vm = pl.BlockSpec(memory_space=pltpu.VMEM)
    anyspace = pl.BlockSpec(memory_space=pl.ANY)
    dma = pltpu.SemaphoreType.DMA
    parts = pl.pallas_call(
        comm_kernel,
        out_shape=(
            pltpu.VMEM((2, 256, 1024), f32),
            pltpu.VMEM((2, NF, 32, 128), f32),
            pltpu.VMEM((2, 256, 128), f32),
            pltpu.VMEM((2, 256, 128), f32),
            pltpu.VMEM((2, 128, 128), f32),
        ),
        in_specs=[pl.BlockSpec(memory_space=pltpu.SMEM)] + [anyspace] * 4,
        out_specs=(vm,) * 5,
        scratch_shapes=[
            pltpu.VMEM((512, 256), b16),
            pltpu.VMEM((2, NX, NY, 32, 512), b16),
            pltpu.VMEM((2, 1, 256, 1024), f32),
            pltpu.VMEM((2, 1024, 128), f32),
            pltpu.VMEM((256, 1024), f32),
            pltpu.VMEM((1024, 256), b16),
            pltpu.VMEM((1024, 256), b16),
            pltpu.VMEM((NZ, PIECE, 128), f32),
            pltpu.VMEM((NZ, PIECE, 128), f32),
            pltpu.VMEM((NZ, PIECE, 128), f32),
            pltpu.VMEM((NZ, PIECE, 128), f32),
            pltpu.VMEM((NZ, PIECE, 128), f32),
            pltpu.VMEM((NZ, PIECE, 128), f32),
            pltpu.VMEM((NF, 32, 128), f32),
            pltpu.VMEM((NF, 32, 128), f32),
            pltpu.VMEM((NY, 32, 128), f32),
            pltpu.VMEM((NZ, 32, 128), f32),
            pltpu.VMEM((NF, 4, 128), f32),
            pltpu.VMEM((NF, 4, 128), f32),
            pltpu.VMEM((NF, 4, 128), f32),
            pltpu.VMEM((128, 128), f32),
            dma((5,)),
            dma((7,)), dma((7,)),
            dma((32,)), dma((32,)),
            dma((36,)), dma((36,)),
            dma((36,)), dma((36,)),
            dma((160,)), dma((160,)),
            pltpu.SemaphoreType.REGULAR((5, 2)),
        ],
        compiler_params=pltpu.CompilerParams(
            collective_id=0, has_side_effects=True, vmem_limit_bytes=58 << 20
        ),
        name="exchange",
    )(factor_ranks, inputs, jnp.swapaxes(cotangent, 1, 2), feedback, q_init)
    return pl.pallas_call(
        final_kernel,
        out_shape=(
            jax.ShapeDtypeStruct((2, 256, 128), f32),
            jax.ShapeDtypeStruct((2, 1024, 128), f32),
            jax.ShapeDtypeStruct((2, 1, 256, 1024), f32),
        ),
        in_specs=[vm] * 5,
        out_specs=(anyspace,) * 3,
        scratch_shapes=[pltpu.VMEM((2, 1024, 128), f32), pltpu.VMEM((2, 256, 1024), f32), dma((17,))],
        compiler_params=pltpu.CompilerParams(vmem_limit_bytes=16 << 20),
        name="finish",
    )(*parts)


def solution(mesh):
    torus = Mesh(mesh.devices.reshape(NZ, 2, NX, NY), ("z", "c", "x", "y"))
    placed = (P(DP, FS), P(None, DP, FS), P(None, DP, FS, None), P(), P())
    return jax.shard_map(
        local,
        mesh=torus,
        in_specs=placed,
        out_specs=(P(None, FS, None), P(), P(None, DP, FS, None)),
        check_vma=False,
    )
```

```python
import functools

import jax
import jax.numpy as jnp
from jax import lax
from jax.experimental import pallas as pl
from jax.experimental.pallas import tpu as pltpu
from jax.sharding import Mesh
from jax.sharding import PartitionSpec as P

MESH = pl.DeviceIdType.MESH
HI = lax.Precision.HIGHEST
NZ, NX, NY = 12, 4, 8
NF = NX * NY
STEPS = (48, 80)
PIECE = 24
DP = ("z", "c")
FS = ("x", "y")

OFFS = sorted(
    [(dx, dy) for dx in range(NX) for dy in range(NY) if dx or dy],
    key=lambda o: -(min(o[0], NX - o[0]) + min(o[1], NY - o[1])),
)
YOFFS = (4, 3, 5, 2, 6, 1, 7)
ZOFFS = sorted(range(1, NZ), key=lambda d: -min(d, NZ - d))


def nt(a, b, precision=HI):
    return lax.dot_general(
        a, b, (((1,), (1,)), ((), ())), precision=precision, preferred_element_type=jnp.float32
    )


def nn(a, b, precision=HI):
    return lax.dot_general(
        a, b, (((1,), (0,)), ((), ())), precision=precision, preferred_element_type=jnp.float32
    )


def split(a):
    high = a.astype(jnp.bfloat16)
    return high, (a - high.astype(jnp.float32)).astype(jnp.bfloat16)


def three(dot, a, b):
    (ah, al), (bh, bl) = a, b
    return dot(ah, bh, None) + (dot(ah, bl, None) + dot(al, bh, None))


def comm_kernel(
    ranks, x_hbm, cot_hbm, fb_hbm, q_hbm,
    g_out, s_out, p_out, r_out, li_out,
    xb, xt, ct, fb, qv, gx, cf_h, cf_l, pp, pq, pr, rs, pf3, pf_x, s_src, s_rs, s_t, s_z, gl, g_rs, gg, mat,
    l_sem, pr_send, pr_recv, a_send, a_recv, b_send, b_recv, z_send, z_recv, f_send, f_recv, near,
):
    z, c, x, y = (lax.axis_index(n) for n in ("z", "c", "x", "y"))
    oc = 1 - c
    f = x * NY + y
    pending = []

    def at(dz=0, dx=0, dy=0):
        return (lax.rem(z + dz, NZ), c, lax.rem(x + dx, NX), lax.rem(y + dy, NY))

    partner = (z, oc, x, y)

    def send(src, dst, ssem, rsem, dev):
        cp = pltpu.make_async_remote_copy(
            src_ref=src, dst_ref=dst, send_sem=ssem, recv_sem=rsem, device_id=dev, device_id_type=MESH
        )
        cp.start()
        pending.append(cp)

    def settle(count=None):
        for cp in pending[:count]:
            cp.wait_send()
        del pending[:count]

    def batch(src, dst, sems, k, dev):
        pltpu.make_async_remote_copy(
            src_ref=src, dst_ref=dst, send_sem=sems[0].at[k], recv_sem=sems[1].at[k], device_id=dev, device_id_type=MESH
        ).start()

    def whole(ref, sems, k):
        return pltpu.make_async_remote_copy(
            src_ref=ref, dst_ref=ref, send_sem=sems[0].at[k], recv_sem=sems[1].at[k],
            device_id=partner, device_id_type=MESH,
        )

    def arrive(dst, ssem, rsem, dev):
        pltpu.make_async_remote_copy(
            src_ref=dst, dst_ref=dst, send_sem=ssem, recv_sem=rsem, device_id=dev, device_id_type=MESH
        ).wait_recv()

    barrier = pltpu.get_barrier_semaphore()
    peers = [partner] + [at(dx=dx) for dx in (1, 2, 3)]
    peers += [at(dy=1), at(dy=NY - 1), at(dz=1), at(dz=NZ - 1)]
    for peer in peers:
        pl.semaphore_signal(barrier, inc=1, device_id=peer, device_id_type=MESH)

    loads = [
        pltpu.make_async_copy(src, dst, l_sem.at[i])
        for i, (src, dst) in enumerate(
            [(cot_hbm.at[r], ct.at[r, x, y]) for r in range(2)] + [(x_hbm, xb), (fb_hbm, fb), (q_hbm, qv)]
        )
    ]
    for cp in loads:
        cp.start()
    for cp in loads[:2]:
        cp.wait()

    pl.semaphore_wait(barrier, len(peers))

    def tell(r):
        for n, dz in enumerate((1, NZ - 1)):
            pl.semaphore_signal(near.at[r - 1, n], inc=1, device_id=at(dz=dz), device_id_type=MESH)

    def told(r):
        for n in range(2):
            pl.semaphore_wait(near.at[r - 1, n], 1)

    def chunk(r, dx, dy):
        return ct.at[r, lax.rem(x + dx + NX, NX), lax.rem(y + dy + NY, NY)]

    def a_y(dirn, s):
        k = chunk(0, 0, -dirn * (s - 1))
        i = (s - 1) if dirn > 0 else 3 + s
        send(k, k, a_send.at[i], a_recv.at[i], at(dy=dirn % NY))

    def a_y_wait(dirn, s):
        i = (s - 1) if dirn > 0 else 3 + s
        arrive(chunk(0, 0, -dirn * s), a_send.at[i], a_recv.at[i], at(dy=-dirn % NY))

    def a_x(j, dirn):
        k = chunk(0, 0, -j)
        i = 8 + j * 3 + (0 if dirn > 0 else 1)
        send(k, k, a_send.at[i], a_recv.at[i], at(dx=dirn % NX))

    def a_x_wait(j, dirn):
        i = 8 + j * 3 + (0 if dirn > 0 else 1)
        arrive(chunk(0, -dirn, -j), a_send.at[i], a_recv.at[i], at(dx=-dirn % NX))

    def far_dir(j):
        return 1 if j % 2 == 0 else -1

    def a_x_far(j):
        d = far_dir(j)
        k = chunk(0, -d, -j)
        i = 8 + j * 3 + 2
        send(k, k, a_send.at[i], a_recv.at[i], at(dx=d % NX))

    def a_x_far_wait(j):
        d = far_dir(j)
        i = 8 + j * 3 + 2
        arrive(chunk(0, -2 * d, -j), a_send.at[i], a_recv.at[i], at(dx=-d % NX))

    def b_x(dx):
        k = chunk(1, 0, 0)
        send(k, k, b_send.at[dx], b_recv.at[dx], at(dx=dx))

    def b_x_wait(dx):
        arrive(chunk(1, -dx, 0), b_send.at[dx], b_recv.at[dx], at(dx=NX - dx))

    def b_reach(dx, dirn):
        return (4 if dirn > 0 else 3) if dx % 2 == 0 else (3 if dirn > 0 else 4)

    def b_idx(dx, dirn, s):
        return 4 + dx * 8 + (s - 1 if dirn > 0 else 3 + s)

    def b_y(dx, dirn, s):
        k = chunk(1, -dx, -dirn * (s - 1))
        i = b_idx(dx, dirn, s)
        send(k, k, b_send.at[i], b_recv.at[i], at(dy=dirn % NY))

    def b_y_wait(dx, dirn, s):
        i = b_idx(dx, dirn, s)
        arrive(chunk(1, -dx, -dirn * s), b_send.at[i], b_recv.at[i], at(dy=-dirn % NY))

    a_y(1, 1)
    a_y(-1, 1)
    a_x(0, 1)
    a_x(0, -1)

    for dx in (1, 3, 2):
        b_x(dx)
    b_y(0, 1, 1)
    b_y(0, -1, 1)
    tell(1)

    def a_hop(s):
        for dirn, last in ((1, 4), (-1, 3)):
            if s <= last:
                a_y_wait(dirn, s)
                if s < last:
                    a_y(dirn, s + 1)
        for j in (s, NY - s) if s < 4 else (4,):
            if s > 2:
                k = chunk(0, 0, -j)
                send(k, k, a_send.at[8 + j * 3 + 2], a_recv.at[8 + j * 3 + 2], at(dx=2))
            a_x(j, 1)
            a_x(j, -1)

    def a_far(j):
        d = far_dir(j)
        a_x_wait(j, d)
        if j not in (3, 4, 5):
            a_x_far(j)
        a_x_wait(j, -d)

    def b_hop(s, dxs):
        for dx in dxs:
            for dirn in (1, -1):
                if s <= b_reach(dx, dirn):
                    b_y_wait(dx, dirn, s)
                    if s < b_reach(dx, dirn):
                        b_y(dx, dirn, s + 1)

    loads[2].wait()
    xt[...] = xb[...].astype(jnp.float32).T.astype(jnp.bfloat16)
    a_hop(1)
    for dx in (1, 3, 2):
        b_x_wait(dx)
        b_y(dx, 1, 1)
        b_y(dx, -1, 1)
    for s in range(1, 5):
        b_hop(s, (0,))
        told(s)
        tell(s + 1)
        if s < 4:
            a_hop(s + 1)
        b_hop(s, (1, 3, 2))
        for j in {1: (0,), 2: (1, 7), 3: (2, 6), 4: (3, 5, 4)}[s]:
            a_far(j)
    told(5)
    for cp in loads[3:]:
        cp.wait()
    for j in (0, 1, 7, 2, 6, 3, 5, 4):
        a_x_far_wait(j)

    width = lax.broadcasted_iota(jnp.int32, (1, 128), 1)
    rank = ranks[c]
    for m, out in ((oc, pq), (c, pp)):
        live = width < ranks[m]
        total = jnp.zeros((256, 128), jnp.float32)
        for b in range(NX):
            cols = pl.ds(b * 256, 256)
            full = fb[m, 0, :, cols] + nt(xt[...], ct[m, b].reshape(256, 512), None)
            g_out[m, :, cols] = full
            total = total + three(nn, split(full), split(jnp.where(live, qv[m, cols, :], 0.0)))
        for i in range(NZ):
            lo, hi = i * PIECE, min((i + 1) * PIECE, 256)
            if hi - lo == PIECE:
                out[i] = total[lo:hi]
            elif hi > lo:
                out[i, : hi - lo] = total[lo:hi]
                out[i, hi - lo :] = jnp.zeros((PIECE - (hi - lo), 128), jnp.float32)
            else:
                out[i] = jnp.zeros((PIECE, 128), jnp.float32)
        if out is pq:
            send(pq, pr, pr_send.at[0], pr_recv.at[0], partner)
    arrive(pr, pr_send.at[0], pr_recv.at[0], partner)
    pp[...] = pp[...] + pr[...]

    sent = len(pending)
    zs_sems = (z_send, z_recv)
    for d in ZOFFS:
        batch(pp.at[lax.rem(z + d, NZ)], rs.at[d], zs_sems, 0, at(dz=d))
    for b in range(4):
        rows = pl.ds(b * 64, 64)
        send(g_out.at[oc, rows], gx.at[rows], pr_send.at[1 + b], pr_recv.at[1 + b], partner)
    settle(sent)
    pieces = whole(rs.at[pl.ds(1, NZ - 1)], zs_sems, 0)
    pieces.wait_recv()
    acc = pp[z]
    for d in range(1, NZ):
        acc = acc + rs[d]
    pf3[z] = acc
    for d in ZOFFS:
        batch(pf3.at[z], pf3.at[z], zs_sems, 1, at(dz=d))
    pieces.wait_send()
    for b in range(4):
        rows = pl.ds(b * 64, 64)
        arrive(gx.at[rows], pr_send.at[1 + b], pr_recv.at[1 + b], partner)
    for b in range(NX):
        cols = pl.ds(b * 256, 256)
        cf_h[cols, :], cf_l[cols, :] = split((g_out[c, :, cols] + gx[:, cols]).T)
    settle()
    pieces = whole(pf3.at[pl.ds(0, NZ - 1)], zs_sems, 1)
    pieces.wait_recv()
    pieces.wait_send()
    left = pf3[...].reshape(NZ * PIECE, 128)[:256]

    f_sems = (f_send, f_recv)
    left_parts = split(left)
    gram = nn(left.T, left)
    for i in range(NF):
        gl[i] = gram[4 * i : 4 * i + 4]
    for n, (dx, dy) in enumerate(OFFS):
        to = lax.rem(x + dx, NX) * NY + lax.rem(y + dy, NY)
        batch(gl.at[to], g_rs.at[n], f_sems, 0, at(dx=dx, dy=dy))
    for b in range(NX):
        rows = pl.ds(b * 256, 256)
        s_src[pl.ds(b * NY, NY)] = three(nn, (cf_h[rows, :], cf_l[rows, :]), left_parts).reshape(NY, 32, 128)
    for dy in YOFFS + (0,):
        for dx in (2, 1, 3):
            to = lax.rem(x + dx, NX) * NY + lax.rem(y + dy, NY)
            i = dx * NY + dy
            send(s_src.at[to], s_rs.at[i], f_send.at[32 + i], f_recv.at[32 + i], at(dx=dx))

    send(pf3, pf_x, pr_send.at[5], pr_recv.at[5], partner)

    def gram_owner():
        pieces = whole(g_rs.at[pl.ds(0, NF - 1)], f_sems, 0)
        pieces.wait_recv()
        acc = gl[f]
        for n in range(NF - 1):
            acc = acc + g_rs[n]
        gg[f] = acc
        for dx, dy in OFFS:
            batch(gg.at[f], gg.at[f], f_sems, 1, at(dx=dx, dy=dy))
        pieces.wait_send()

    for dy in YOFFS + (0,):
        if dy == 2:
            gram_owner()
        acc = s_src[x * NY + lax.rem(y + dy, NY)]
        for dx in (1, 3, 2):
            i = dx * NY + dy
            arrive(s_rs.at[i], f_send.at[32 + i], f_recv.at[32 + i], at(dx=NX - dx))
            acc = acc + s_rs[i]
        if dy:
            s_t[dy] = acc
            batch(s_t.at[dy], s_rs.at[dy], f_sems, 2, at(dy=dy))
    settle()
    pieces = whole(s_rs.at[pl.ds(1, NY - 1)], f_sems, 2)
    pieces.wait_recv()
    for dy in range(1, NY):
        acc = acc + s_rs[dy]
    s_z[z] = acc
    for d in ZOFFS:
        batch(s_z.at[z], s_z.at[z], zs_sems, 2, at(dz=d))
    pieces.wait_send()

    pieces = whole(gg.at[pl.ds(0, NF - 1)], f_sems, 1)
    pieces.wait_recv()
    pieces.wait_send()
    for i in range(NF):
        mat[4 * i : 4 * i + 4, :] = gg[i]
    row_id = lax.broadcasted_iota(jnp.int32, (128, 128), 0)
    col_id = lax.broadcasted_iota(jnp.int32, (128, 128), 1)
    mat[...] = mat[...] + jnp.where((row_id == col_id) & (col_id >= rank), 1.0, 0.0)

    def eliminate(j, carry):
        m = mat[...]
        row = mat[pl.ds(j, 1), :]
        hit = col_id == j
        hit1 = width == j
        pivot = jnp.sum(jnp.where(hit1, row, 0.0), axis=1, keepdims=True)
        col = jnp.sum(jnp.where(hit, m, 0.0), axis=1, keepdims=True)
        factor = jnp.where(row_id > j, col / pivot, 0.0)
        mat[...] = jnp.where(hit & (row_id > j), 0.0, m) - factor * jnp.where(hit1, 1.0, row)
        return carry

    lax.fori_loop(0, STEPS[0], eliminate, 0)

    pieces = whole(s_z.at[pl.ds(0, NZ - 1)], zs_sems, 2)
    pieces.wait_recv()
    pieces.wait_send()
    acc = s_z[0]
    for i in range(1, NZ):
        acc = acc + s_z[i]
    s_out[c, f] = acc

    def piece(dx, dy):
        return lax.rem(x + NX - dx, NX) * NY + lax.rem(y + NY - dy, NY)

    def forward(dx, dy):
        k = piece(dx, dy)
        batch(s_out.at[c, k], s_out.at[c, k], f_sems, 3, partner)

    def spread(dy):
        k = piece(0, dy)
        for dx in (2, 1, 3):
            i = 96 + dx * NY + dy
            send(s_out.at[c, k], s_out.at[c, k], f_send.at[i], f_recv.at[i], at(dx=dx))
        forward(0, dy)

    for dy in YOFFS:
        send(s_out.at[c, f], s_out.at[c, f], f_send.at[96 + dy], f_recv.at[96 + dy], at(dy=dy))
    spread(0)
    lax.fori_loop(STEPS[0], STEPS[1], eliminate, 0)
    for dy in reversed(YOFFS):
        arrive(s_out.at[c, piece(0, dy)], f_send.at[96 + dy], f_recv.at[96 + dy], at(dy=NY - dy))
        spread(dy)

    lax.fori_loop(STEPS[1], 128, eliminate, 0)
    m = mat[...]
    diag = jnp.sum(jnp.where(row_id == col_id, m, 0.0), axis=1, keepdims=True)
    unit = jnp.where(row_id == col_id, 1.0, jnp.where(row_id > col_id, m, 0.0))
    li_out[c] = unit * (1.0 / jnp.sqrt(diag))
    send(li_out.at[c], li_out.at[c], pr_send.at[6], pr_recv.at[6], partner)

    def factor(m, parts):
        inv = split(li_out[m])
        own = three(nt, parts, inv)
        p_out[m] = own
        r_out[m] = three(nn, split(own), inv)

    factor(c, left_parts)
    settle()
    for dy in (0,) + YOFFS[::-1]:
        for dx in (1, 3, 2):
            i = 96 + dx * NY + dy
            arrive(s_out.at[c, piece(dx, dy)], f_send.at[i], f_recv.at[i], at(dx=NX - dx))
            forward(dx, dy)
    arrive(pf_x, pr_send.at[5], pr_recv.at[5], partner)
    arrive(li_out.at[oc], pr_send.at[6], pr_recv.at[6], partner)
    factor(oc, split(pf_x[...].reshape(NZ * PIECE, 128)[:256]))
    pieces = whole(s_out.at[oc], f_sems, 3)
    pieces.wait_recv()
    pieces.wait_send()


def final_kernel(g, s, p, r, li, p_out, q_out, e_out, q_buf, e_buf, sem):
    puts = []

    def put(src, dst):
        puts.append(pltpu.make_async_copy(src, dst, sem.at[len(puts)]))
        puts[-1].start()

    put(p, p_out)
    for m in range(2):
        inv, right = split(li[m]), split(r[m])
        for b in range(NX):
            cols = pl.ds(b * 256, 256)
            raw = split(s[m, b * NY : (b + 1) * NY].reshape(256, 128))
            e_buf[m, :, cols] = g[m, :, cols] - three(nt, right, raw)
            put(e_buf.at[m, :, cols], e_out.at[m, 0, :, cols])
            q_buf[m, cols, :] = three(nt, raw, inv)
            put(q_buf.at[m, cols, :], q_out.at[m, cols, :])
    for cp in puts:
        cp.wait()


def local(inputs, cotangent, feedback, q_init, factor_ranks):
    f32, b16 = jnp.float32, jnp.bfloat16
    vm = pl.BlockSpec(memory_space=pltpu.VMEM)
    anyspace = pl.BlockSpec(memory_space=pl.ANY)
    dma = pltpu.SemaphoreType.DMA
    parts = pl.pallas_call(
        comm_kernel,
        out_shape=(
            pltpu.VMEM((2, 256, 1024), f32),
            pltpu.VMEM((2, NF, 32, 128), f32),
            pltpu.VMEM((2, 256, 128), f32),
            pltpu.VMEM((2, 256, 128), f32),
            pltpu.VMEM((2, 128, 128), f32),
        ),
        in_specs=[pl.BlockSpec(memory_space=pltpu.SMEM)] + [anyspace] * 4,
        out_specs=(vm,) * 5,
        scratch_shapes=[
            pltpu.VMEM((512, 256), b16),
            pltpu.VMEM((256, 512), b16),
            pltpu.VMEM((2, NX, NY, 32, 512), b16),
            pltpu.VMEM((2, 1, 256, 1024), f32),
            pltpu.VMEM((2, 1024, 128), f32),
            pltpu.VMEM((256, 1024), f32),
            pltpu.VMEM((1024, 256), b16),
            pltpu.VMEM((1024, 256), b16),
            pltpu.VMEM((NZ, PIECE, 128), f32),
            pltpu.VMEM((NZ, PIECE, 128), f32),
            pltpu.VMEM((NZ, PIECE, 128), f32),
            pltpu.VMEM((NZ, PIECE, 128), f32),
            pltpu.VMEM((NZ, PIECE, 128), f32),
            pltpu.VMEM((NZ, PIECE, 128), f32),
            pltpu.VMEM((NF, 32, 128), f32),
            pltpu.VMEM((NF, 32, 128), f32),
            pltpu.VMEM((NY, 32, 128), f32),
            pltpu.VMEM((NZ, 32, 128), f32),
            pltpu.VMEM((NF, 4, 128), f32),
            pltpu.VMEM((NF, 4, 128), f32),
            pltpu.VMEM((NF, 4, 128), f32),
            pltpu.VMEM((128, 128), f32),
            dma((5,)),
            dma((7,)), dma((7,)),
            dma((32,)), dma((32,)),
            dma((36,)), dma((36,)),
            dma((36,)), dma((36,)),
            dma((160,)), dma((160,)),
            pltpu.SemaphoreType.REGULAR((5, 2)),
        ],
        compiler_params=pltpu.CompilerParams(
            collective_id=0, has_side_effects=True, vmem_limit_bytes=58 << 20
        ),
        name="exchange",
    )(factor_ranks, inputs, jnp.swapaxes(cotangent, 1, 2), feedback, q_init)
    return pl.pallas_call(
        final_kernel,
        out_shape=(
            jax.ShapeDtypeStruct((2, 256, 128), f32),
            jax.ShapeDtypeStruct((2, 1024, 128), f32),
            jax.ShapeDtypeStruct((2, 1, 256, 1024), f32),
        ),
        in_specs=[vm] * 5,
        out_specs=(anyspace,) * 3,
        scratch_shapes=[pltpu.VMEM((2, 1024, 128), f32), pltpu.VMEM((2, 256, 1024), f32), dma((17,))],
        compiler_params=pltpu.CompilerParams(vmem_limit_bytes=16 << 20),
        name="finish",
    )(*parts)


def solution(mesh):
    torus = Mesh(mesh.devices.reshape(NZ, 2, NX, NY), ("z", "c", "x", "y"))
    placed = (P(DP, FS), P(None, DP, FS), P(None, DP, FS, None), P(), P())
    return jax.shard_map(
        local,
        mesh=torus,
        in_specs=placed,
        out_specs=(P(None, FS, None), P(), P(None, DP, FS, None)),
        check_vma=False,
    )
```
